256 devices in a mesh: coarse: 8 (over x, core), fine: 32 (over z, y).
Axes of the slice: x: 4, y: 4, z: 8, core: 2. Of those that a mesh axis runs over, the one named last changes fastest.
Arguments:
- tokens: bfloat16 [131072, 1024], P(('coarse', 'fine'))
- w_qkv: bfloat16 [1024, 3072], replicated, may hold values from -0.1875 to 0.1875
- w_coarse_out: bfloat16 [1024, 1024], replicated, may hold values from -0.1875 to 0.1875
- w_kv2: bfloat16 [1024, 2048], replicated, may hold values from -0.1875 to 0.1875
- w_out: bfloat16 [1024, 1024], replicated, may hold values from -0.1875 to 0.1875
- seg_start: int32 [4096], P('coarse'), may hold values from 0 to 131071, as said below
- seg_end: int32 [4096], P('coarse'), may hold values from 1 to 131072, as said below
- block_lists: int32 [512, 8], P(('coarse', 'fine')), may hold values from 0 to 255, as said below
Outputs:
- mixed: bfloat16 [131072, 1024], P(('coarse', 'fine'))
The draws below stay inside these ranges and needn't reach their ends.
Inputs may be any that keep to these rules, and one draw needn't show every extreme that they name: `seg_start`: for each coarse owner c, the segments c*512 to (c+1)*512 - 1 are nonempty and pairwise disjoint and lie within time steps c*16384 to (c+1)*16384 - 1, listed in an order that does not follow time; steps outside all segments belong to none; segment lengths are uneven. seg_end[s] > seg_start[s]. `block_lists`: row n names 8 distinct coarse key blocks (block b holds segments b*16 to (b+1)*16 - 1), all among the blocks of owners c-1, c and c+1 taken cyclically over the owners, where c = n*256 // 16384 is the owner of the row's time steps.
All inputs are finite; a program needn't handle non-finite values.
Results may differ from the reference program's by a relative error of at most 0.017.
Values may be sent and summed in bfloat16 or wider, within the bound.
A program may use at most 128 MiB of HBM per device.

```python
import math
import jax
import jax.numpy as jnp
from jax import lax

D = 1024
HEADS = 8
TOK_DEV = 512
KB = 16
QB = 256
NBL = 8
STEP_COUNT_ALL = 131072
SPAN = 16384
SEG_OWN = 512
NSEG = 4096
WC = 256
NQB = 512
N_COARSE = 8
N_FINE = 32


def segment_table(key):
    base_key = jax.random.fold_in(key, 7)
    owner_keys = jax.random.split(base_key, N_COARSE)

    def one_owner(owner_key):
        cut_key, trim_key, order_key = jax.random.split(owner_key, 3)
        shuffled = jax.random.permutation(cut_key, SPAN - 1).astype(jnp.int32)
        cuts = jnp.sort(shuffled[:SEG_OWN - 1] + 1)
        starts = jnp.concatenate([jnp.zeros((1,), jnp.int32), cuts])
        limits = jnp.concatenate([cuts, jnp.full((1,), SPAN, jnp.int32)])
        spans = limits - starts
        trims = jax.random.randint(trim_key, (SEG_OWN,), 0, spans // 2 + 1).astype(jnp.int32)
        ends = starts + spans - trims
        order = jax.random.permutation(order_key, SEG_OWN).astype(jnp.int32)
        return (jnp.take(starts, order), jnp.take(ends, order))
    starts, ends = jax.vmap(one_owner)(owner_keys)
    offsets = jnp.arange(N_COARSE, dtype=jnp.int32)[:, None] * SPAN
    return ((starts + offsets).reshape(NSEG), (ends + offsets).reshape(NSEG))


def draw_seg_start(key, part):
    return segment_table(key)[0]


def draw_seg_end(key, part):
    return segment_table(key)[1]


def draw_block_lists(key, part):
    choices_per_row = 3 * N_FINE
    scores = jax.random.randint(jax.random.fold_in(key, 11), (NQB, choices_per_row), 0, 1 << 20).astype(jnp.int32)
    scores = scores * choices_per_row + jnp.arange(choices_per_row, dtype=jnp.int32)[None, :]
    picks = jnp.argsort(scores, axis=1)[:, :NBL].astype(jnp.int32)
    owner = jnp.arange(NQB, dtype=jnp.int32) * QB // SPAN
    blocks = owner[:, None] * N_FINE - N_FINE + picks
    return jnp.mod(blocks, N_COARSE * N_FINE).astype(jnp.int32)


def draw_tokens(key, part):
    first_key = jax.random.fold_in(jax.random.fold_in(key, 3), 0)
    content_elements = jax.random.normal(first_key, (STEP_COUNT_ALL, D), jnp.float32)
    return jnp.clip(content_elements, -60.0, 60.0).astype(jnp.bfloat16)


def normal_values(key, dims, width, limit, kind=jnp.bfloat16):
    entries = jax.random.normal(key, dims, jnp.float32) * width
    return jnp.minimum(jnp.maximum(entries, -limit), limit).astype(kind)


def setup_inputs(seed: int = 0) -> dict:
    key_of = jax.random.split(jax.random.key(seed), 9)
    tokens = draw_tokens(jax.random.fold_in(key_of[8], 71), 0)
    w_qkv = normal_values(key_of[1], (D, 3 * D), D ** -0.5, 0.1875)
    w_coarse_out = normal_values(key_of[2], (D, D), D ** -0.5, 0.1875)
    w_kv2 = normal_values(key_of[3], (D, 2 * D), D ** -0.5, 0.1875)
    w_out = normal_values(key_of[4], (D, D), D ** -0.5, 0.1875)
    seg_start = draw_seg_start(jax.random.fold_in(key_of[8], 71), 0)
    seg_end = draw_seg_end(jax.random.fold_in(key_of[8], 71), 0)
    block_lists = draw_block_lists(jax.random.fold_in(key_of[8], 71), 0)
    return {"tokens": tokens, "w_qkv": w_qkv, "w_coarse_out": w_coarse_out, "w_kv2": w_kv2, "w_out": w_out, "seg_start": seg_start, "seg_end": seg_end, "block_lists": block_lists}


def attend_heads(queries, keys, content_elements, allowed):
    count = queries.shape[0]
    head_size = queries.shape[1] // HEADS
    query_heads = queries.astype(jnp.float32).reshape(count, HEADS, head_size)
    key_heads = keys.astype(jnp.float32).reshape(keys.shape[0], HEADS, head_size)
    value_heads = content_elements.astype(jnp.float32).reshape(content_elements.shape[0], HEADS, head_size)
    scores = jnp.einsum('qhd,khd->hqk', query_heads, key_heads) * (1.0 / math.sqrt(head_size))
    scores = jnp.where(allowed[None], scores, -1e+30)
    highest = lax.optimization_barrier(jnp.max(scores, axis=-1, keepdims=True))
    expos = jnp.exp(scores - highest)
    weights = (expos / lax.optimization_barrier(jnp.sum(expos, axis=-1, keepdims=True))).astype(jnp.bfloat16)
    blended = jnp.einsum('hqk,khd->qhd', weights.astype(jnp.float32), value_heads)
    return blended.astype(jnp.bfloat16).reshape(count, HEADS * head_size)

def normalize(content_elements):
    return content_elements * lax.rsqrt(lax.optimization_barrier(jnp.mean(content_elements * content_elements, axis=-1, keepdims=True)) + 1e-06)

def reference(tokens, w_qkv, w_coarse_out, w_kv2, w_out, seg_start, seg_end, block_lists):

    def pool_owner(owner):
        rows = lax.dynamic_slice_in_dim(tokens, owner * SPAN, SPAN, 0)
        starts = lax.dynamic_slice_in_dim(seg_start, owner * SEG_OWN, SEG_OWN, 0)
        ends = lax.dynamic_slice_in_dim(seg_end, owner * SEG_OWN, SEG_OWN, 0)
        places = owner * SPAN + jnp.arange(SPAN, dtype=jnp.int32)
        member = ((places[None, :] >= starts[:, None]) & (places[None, :] < ends[:, None])).astype(jnp.bfloat16)
        return jnp.dot(member, rows, preferred_element_type=jnp.float32)
    sums = lax.map(pool_owner, jnp.arange(N_COARSE, dtype=jnp.int32)).reshape(NSEG, D)
    spans = (seg_end - seg_start).astype(jnp.float32)
    pooled = (sums / jnp.sqrt(spans)[:, None]).astype(jnp.bfloat16)
    coarse_proj = jnp.dot(pooled, w_qkv, preferred_element_type=jnp.float32)
    coarse_query = coarse_proj[:, :D].astype(jnp.bfloat16)
    coarse_key = coarse_proj[:, D:2 * D].astype(jnp.bfloat16)
    coarse_value = coarse_proj[:, 2 * D:].astype(jnp.bfloat16)
    places = jnp.arange(NSEG, dtype=jnp.int32)
    apart = jnp.abs(places[:, None] - places[None, :])
    allowed = jnp.minimum(apart, NSEG - apart) <= WC
    coarse_mix = attend_heads(coarse_query, coarse_key, coarse_value, allowed)
    context = jnp.dot(coarse_mix, w_coarse_out, preferred_element_type=jnp.float32)
    state = normalize(context).astype(jnp.bfloat16)
    second = jnp.dot(state, w_kv2, preferred_element_type=jnp.float32).astype(jnp.bfloat16)
    per_device = TOK_DEV // QB

    def device_rows(device):
        rows = lax.dynamic_slice_in_dim(tokens, device * TOK_DEV, TOK_DEV, 0)
        proj = jnp.dot(rows, w_qkv, preferred_element_type=jnp.float32)
        query = proj[:, :D].astype(jnp.bfloat16)
        key_rows = proj[:, D:2 * D].astype(jnp.bfloat16)
        value_rows = proj[:, 2 * D:].astype(jnp.bfloat16)
        lists = lax.dynamic_slice_in_dim(block_lists, device * per_device, per_device, 0)

        def query_block(number):
            block_query = lax.dynamic_slice_in_dim(query, number * QB, QB, 0)
            listed = lax.dynamic_index_in_dim(lists, number, 0, keepdims=False)
            picked = (listed[:, None] * KB + jnp.arange(KB, dtype=jnp.int32)[None, :]).reshape(-1)
            remote = jnp.take(second, picked, axis=0)
            keys = jnp.concatenate([key_rows, remote[:, :D]], axis=0)
            content_elements = jnp.concatenate([value_rows, remote[:, D:]], axis=0)
            allowed_all = jnp.ones((QB, keys.shape[0]), dtype=bool)
            return attend_heads(block_query, keys, content_elements, allowed_all)
        attended = lax.map(query_block, jnp.arange(per_device, dtype=jnp.int32)).reshape(TOK_DEV, D)
        projected = jnp.dot(attended, w_out, preferred_element_type=jnp.float32)
        return normalize(projected).astype(jnp.bfloat16)
    mixed = lax.map(device_rows, jnp.arange(N_COARSE * N_FINE, dtype=jnp.int32))
    return mixed.reshape(STEP_COUNT_ALL, D)
```

```python
import math

import jax
import jax.numpy as jnp
from jax import lax
from jax.experimental import pallas as pl
from jax.experimental.pallas import tpu as pltpu
from jax.sharding import PartitionSpec as P

HEADS = 8
KB = 16
QB = 256
NY = 4
NZ = 8
NC = 8
D = 1024
HS = 128
ROWS = 512
SEGS = 512
REACH = 256
SCALE = 1.0 / math.sqrt(HS)
SCALE2 = SCALE * math.log2(math.e)
BF = jnp.bfloat16
F32 = jnp.float32
NT = (((1,), (1,)), ((), ()))
MESH = pl.DeviceIdType.MESH


def dot(a, b):
    return jnp.dot(a, b, preferred_element_type=F32)


def dot_nt(a, b):
    return lax.dot_general(a, b, NT, preferred_element_type=F32)


def normalize(x):
    return x * lax.rsqrt(jnp.mean(x * x, axis=-1, keepdims=True) + 1e-06)


def kernel(
    seg_ref, pick_ref, tok_hbm, wqkv_hbm, wco_hbm, wkv2_hbm, wout_hbm, out_ref,
    tok, wqkv, wco, wkv2, wout, part, ra, rb, sab, r2, red, rz, t1, t2, qkv, acc, mloc, lloc,
    qk, gath, kv2, att, load_sem, send_sem, recv_sem,
):
    c = lax.axis_index("coarse")
    f = lax.axis_index("fine")
    z = f // NY
    y = f % NY
    ya = y + 1 - 2 * (y % 2)
    yb = 3 - y
    yc = (y + 2) % 4
    up = (c + 1) % NC
    down = (c + NC - 1) % NC

    loads = [
        pltpu.make_async_copy(src, dst, load_sem.at[i])
        for i, (src, dst) in enumerate(
            ((tok_hbm, tok), (wqkv_hbm, wqkv), (wco_hbm, wco), (wkv2_hbm, wkv2), (wout_hbm, wout))
        )
    ]
    for load in loads:
        load.start()

    at_y = lambda yy: {"fine": z * NY + yy}
    at_z = lambda zz: {"fine": zz * NY + y}
    at_c = lambda cc: {"coarse": cc}

    barrier = pltpu.get_barrier_semaphore()
    peers = [at_z((z + dz) % NZ) for dz in range(1, NZ)]
    peers += [at_y(ya), at_y(yb), at_c(up), at_c(down)]
    for peer in peers:
        pl.semaphore_signal(barrier, inc=1, device_id=peer, device_id_type=MESH)

    counter = [0]

    def send(src, dst, where):
        k = counter[0]
        counter[0] = k + 1
        copy = pltpu.make_async_remote_copy(
            src_ref=src, dst_ref=dst, send_sem=send_sem.at[k], recv_sem=recv_sem.at[k],
            device_id=where, device_id_type=MESH,
        )
        copy.start()
        copies.append(copy)
        return copy

    copies = []
    first_row = (c * (NY * NZ) + f) * ROWS

    def partial(yy):
        rows = pl.ds(pl.multiple_of(yy * 128, 128), 128)
        low = seg_ref[rows, 0:1] - first_row
        high = seg_ref[rows, 1:2] - first_row
        place = lax.broadcasted_iota(jnp.int32, (128, ROWS), 1)
        member = jnp.where((place >= low) & (place < high), 1.0, 0.0).astype(BF)
        part[yy] = dot(member, tok[...]).astype(BF).reshape(NZ, KB, D)

    lo = pl.ds(0, 4)
    hi = pl.ds(4, 4)
    loads[0].wait()
    partial(yc)
    pl.semaphore_wait(barrier, len(peers))
    a1 = send(part.at[yc, lo], ra.at[1], at_y(ya))
    b1 = send(part.at[yc, hi], rb.at[1], at_y(yb))
    partial(ya)
    a0 = send(part.at[ya, lo], ra.at[0], at_y(ya))
    partial(yb)
    b0 = send(part.at[yb, hi], rb.at[0], at_y(yb))
    partial(y)

    def project(j, carry):
        cols = pl.ds(pl.multiple_of(j * 256, 256), 256)
        qkv[:, cols] = dot(tok[...], wqkv[:, cols]).astype(BF)
        return carry

    loads[1].wait()
    lax.fori_loop(0, 6, project, 0)

    a1.wait_recv()
    sab[0] = (part[yb, 0:4].astype(F32) + ra[1].astype(F32)).astype(BF)
    a2 = send(sab.at[0], r2.at[0], at_y(yb))
    b1.wait_recv()
    sab[1] = (part[ya, 4:8].astype(F32) + rb[1].astype(F32)).astype(BF)
    b2 = send(sab.at[1], r2.at[1], at_y(ya))
    lax.fori_loop(6, 12, project, 0)
    a0.wait_recv()
    a2.wait_recv()
    red[0:4] = (part[y, 0:4].astype(F32) + ra[0].astype(F32) + r2[0].astype(F32)).astype(BF)
    b0.wait_recv()
    b2.wait_recv()
    red[4:8] = (part[y, 4:8].astype(F32) + rb[0].astype(F32) + r2[1].astype(F32)).astype(BF)
    order = (4, 3, 5, 2, 6, 1, 7)
    zs = [send(red.at[(z + dz) % NZ], rz.at[dz - 1], at_z((z + dz) % NZ)) for dz in order]

    def local(it, carry):
        rows = pl.ds(pl.multiple_of((it // HEADS) * QB, QB), QB)
        col = (it % HEADS) * HS
        cols = pl.ds(pl.multiple_of(col, HS), HS)
        keys = qkv[:, pl.ds(pl.multiple_of(col + D, HS), HS)]
        vals = qkv[:, pl.ds(pl.multiple_of(col + 2 * D, HS), HS)]
        s = dot_nt(qkv[rows, cols], keys)
        m = jnp.max(s, axis=1, keepdims=True)
        p = jnp.exp2((s - m) * SCALE2)
        lloc[it] = jnp.sum(p, axis=1, keepdims=True)
        mloc[it] = m
        acc[rows, cols] = dot(p.astype(BF), vals)
        return carry

    lax.fori_loop(0, 8, local, 0)

    for copy in zs:
        copy.wait_recv()
    total = red[z].astype(F32)
    for dz in range(1, NZ):
        total = total + rz[dz - 1].astype(F32)
    mine = seg_ref[pl.ds(pl.multiple_of((y * NZ + z) * KB, KB), KB), :]
    span = (mine[:, 1:2] - mine[:, 0:1]).astype(F32)
    pooled = (total / jnp.sqrt(span)).astype(BF)
    t1[4 + z, y] = pooled

    def gather(table, base, own_first, work):
        zc = [
            send(table.at[base + z, y], table.at[base + z, y], at_z((z + dz) % NZ)) for dz in order
        ]
        work[0]()
        for copy in zc:
            copy.wait_recv()
        low = pl.ds(base, 4)
        high = pl.ds(base + 4, 4)
        ups = high if own_first else pl.ds(base, 8)
        downs = low if own_first else pl.ds(base, 8)
        size = 4 if own_first else 8
        top = 12 if own_first else 16
        halo = []

        def to_owners(yy):
            halo.append(send(table.at[ups, yy], table.at[pl.ds(0, size), yy], at_c(up)))
            halo.append(send(table.at[downs, yy], table.at[pl.ds(top, size), yy], at_c(down)))

        y1 = send(table.at[low, y], table.at[low, y], at_y(ya))
        y2 = send(table.at[high, y], table.at[high, y], at_y(yb))
        y3 = send(table.at[low, y], table.at[low, y], at_y(yb))
        y4 = send(table.at[high, y], table.at[high, y], at_y(ya))
        to_owners(y)
        work[1]()
        y1.wait_recv()
        y5 = send(table.at[low, ya], table.at[low, ya], at_y(yb))
        y2.wait_recv()
        y6 = send(table.at[high, yb], table.at[high, yb], at_y(ya))
        y4.wait_recv()
        to_owners(ya)
        y3.wait_recv()
        to_owners(yb)
        y5.wait_recv()
        y6.wait_recv()
        to_owners(yc)
        work[2]()
        for copy in halo:
            copy.wait_recv()

    def absorb():
        query = dot(pooled, wqkv[:, 0:D]).astype(BF)
        for h in range(HEADS):
            qk[h * KB:(h + 1) * KB] = dot_nt(
                query[:, h * HS:(h + 1) * HS], wqkv[:, D + h * HS:D + (h + 1) * HS]
            ).astype(BF)

    gather(
        t1, 4, True,
        (absorb, lambda: lax.fori_loop(8, 12, local, 0), lambda: lax.fori_loop(12, 16, local, 0)),
    )

    table = t1[...].reshape(1024, D)
    s = dot_nt(qk[...], table)
    row = lax.broadcasted_iota(jnp.int32, s.shape, 0) % KB + f * KB
    key = lax.broadcasted_iota(jnp.int32, s.shape, 1) - REACH
    s = jnp.where(jnp.abs(row - key) <= REACH, s, -1e30)
    m = jnp.max(s, axis=1, keepdims=True)
    p = jnp.exp2((s - m) * SCALE2)
    w = (p / jnp.sum(p, axis=1, keepdims=True)).astype(BF)
    mixed = dot(w, table).astype(BF)
    mix = jnp.concatenate(
        [
            dot(mixed[h * KB:(h + 1) * KB], wqkv[:, 2 * D + h * HS:2 * D + (h + 1) * HS])
            for h in range(HEADS)
        ],
        axis=1,
    ).astype(BF)
    loads[2].wait()
    state = normalize(dot(mix, wco[...])).astype(BF)
    t2[8 + z, y] = state
    nothing = lambda: None
    gather(t2, 8, False, (nothing, nothing, nothing))

    for j in range(16):
        idx = pick_ref[j]
        gath[j * KB:(j + 1) * KB] = t2[idx // NY, idx % NY]
    loads[3].wait()

    def second(j, carry):
        cols = pl.ds(pl.multiple_of(j * 256, 256), 256)
        kv2[:, cols] = dot(gath[...], wkv2[:, cols]).astype(BF)
        return carry

    lax.fori_loop(0, 8, second, 0)

    def remote(it, carry):
        n = it // HEADS
        rows = pl.ds(pl.multiple_of(n * QB, QB), QB)
        col = (it % HEADS) * HS
        cols = pl.ds(pl.multiple_of(col, HS), HS)
        listed = pl.ds(pl.multiple_of(n * 128, 128), 128)
        s = dot_nt(qkv[rows, cols], kv2[listed, cols])
        m0 = mloc[it]
        m = jnp.maximum(m0, jnp.max(s, axis=1, keepdims=True))
        a = jnp.exp2((m0 - m) * SCALE2)
        p = jnp.exp2((s - m) * SCALE2)
        total = a * lloc[it] + jnp.sum(p, axis=1, keepdims=True)
        vals = kv2[listed, pl.ds(pl.multiple_of(col + D, HS), HS)]
        o = acc[rows, cols] * a + dot(p.astype(BF), vals)
        att[rows, cols] = (o / total).astype(BF)
        return carry

    lax.fori_loop(0, 16, remote, 0)
    loads[4].wait()

    def finish(i, carry):
        rows = pl.ds(pl.multiple_of(i * 128, 128), 128)
        out_ref[rows, :] = normalize(dot(att[rows, :], wout[...])).astype(BF)
        return carry

    lax.fori_loop(0, 4, finish, 0)
    for copy in copies:
        copy.wait_send()


COPIES = 4 + 2 + 7 + 2 * (7 + 6 + 8)


def body(tokens, w_qkv, w_coarse_out, w_kv2, w_out, seg_start, seg_end, block_lists):
    seg = jnp.stack([seg_start, seg_end], axis=1).reshape(NZ, NY, KB, 2)
    seg = seg.transpose(1, 0, 2, 3).reshape(SEGS, 2)
    base = (lax.axis_index("coarse") - 1) * (SEGS // KB)
    pick = jnp.mod(block_lists.reshape(-1) - base, NC * SEGS // KB)
    vmem = lambda shape, kind: pltpu.VMEM(shape, kind)
    return pl.pallas_call(
        kernel,
        out_shape=jax.ShapeDtypeStruct((ROWS, D), BF),
        in_specs=[
            pl.BlockSpec(memory_space=pltpu.VMEM),
            pl.BlockSpec(memory_space=pltpu.SMEM),
        ] + [pl.BlockSpec(memory_space=pl.ANY)] * 5,
        out_specs=pl.BlockSpec(memory_space=pltpu.VMEM),
        scratch_shapes=[
            vmem((ROWS, D), BF),
            vmem((D, 3 * D), BF),
            vmem((D, D), BF),
            vmem((D, 2 * D), BF),
            vmem((D, D), BF),
            vmem((NY, NZ, KB, D), BF),
            vmem((2, 4, KB, D), BF),
            vmem((2, 4, KB, D), BF),
            vmem((2, 4, KB, D), BF),
            vmem((2, 4, KB, D), BF),
            vmem((NZ, KB, D), BF),
            vmem((NZ - 1, KB, D), BF),
            vmem((16, NY, KB, D), BF),
            vmem((24, NY, KB, D), BF),
            vmem((ROWS, 3 * D), BF),
            vmem((ROWS, D), F32),
            vmem((16, QB, 1), F32),
            vmem((16, QB, 1), F32),
            vmem((HEADS * KB, D), BF),
            vmem((256, D), BF),
            vmem((256, 2 * D), BF),
            vmem((ROWS, D), BF),
            pltpu.SemaphoreType.DMA((5,)),
            pltpu.SemaphoreType.DMA((COPIES,)),
            pltpu.SemaphoreType.DMA((COPIES,)),
        ],
        compiler_params=pltpu.CompilerParams(
            collective_id=0, has_side_effects=True, vmem_limit_bytes=60 * 1024 * 1024
        ),
    )(seg, pick, tokens, w_qkv, w_coarse_out, w_kv2, w_out)


def solution(mesh):
    placed = (
        P(("coarse", "fine"), None),
        P(),
        P(),
        P(),
        P(),
        P("coarse"),
        P("coarse"),
        P(("coarse", "fine"), None),
    )
    return jax.shard_map(
        body, mesh=mesh, in_specs=placed, out_specs=P(("coarse", "fine"), None), check_vma=False
    )
```

```python
import math

import jax
import jax.numpy as jnp
from jax import lax
from jax.experimental import pallas as pl
from jax.experimental.pallas import tpu as pltpu
from jax.sharding import PartitionSpec as P

HEADS = 8
KB = 16
QB = 256
NY = 4
NZ = 8
NC = 8
D = 1024
HS = 128
ROWS = 512
SEGS = 512
REACH = 256
SCALE = 1.0 / math.sqrt(HS)
SCALE2 = SCALE * math.log2(math.e)
BF = jnp.bfloat16
F32 = jnp.float32
NT = (((1,), (1,)), ((), ()))
MESH = pl.DeviceIdType.MESH


def dot(a, b):
    return jnp.dot(a, b, preferred_element_type=F32)


def dot_nt(a, b):
    return lax.dot_general(a, b, NT, preferred_element_type=F32)


def normalize(x):
    return x * lax.rsqrt(jnp.mean(x * x, axis=-1, keepdims=True) + 1e-06)


OFFS = (0, -1, 1, -2, 2, -3, 3, 4)
COPIES = 31 + 63 + 95


def kernel(
    start_ref, end_ref, list_ref, tok_hbm, wqkv_hbm, wco_hbm, wkv2_hbm, att,
    tok, wqkv, wco, wkv2, scol, ecol, part, rc, rd, re, relay, red, rz, t1, t2, qkv, acc, mloc,
    lloc, qk, gath, kv2, load_sem, send_sem, recv_sem,
):
    c = lax.axis_index("coarse")
    f = lax.axis_index("fine")
    z = f // NY
    y = f % NY
    ya = y + 1 - 2 * (y % 2)
    yb = 3 - y
    yc = (y + 2) % 4
    up = (c + 1) % NC
    down = (c + NC - 1) % NC

    loads = [
        pltpu.make_async_copy(src, dst, load_sem.at[i])
        for i, (src, dst) in enumerate(
            ((tok_hbm, tok), (wqkv_hbm, wqkv), (wco_hbm, wco), (wkv2_hbm, wkv2))
        )
    ]
    for load in loads:
        load.start()

    at_y = lambda yy: {"fine": z * NY + yy}
    at_z = lambda zz: {"fine": zz * NY + y}
    at_c = lambda cc: {"coarse": cc}
    zat = lambda s: (z + s + NZ) % NZ

    barrier = pltpu.get_barrier_semaphore()
    peers = [at_z(zat(s)) for s in OFFS[1:]]
    peers += [at_y(ya), at_y(yb), at_c(up), at_c(down)]
    for peer in peers:
        pl.semaphore_signal(barrier, inc=1, device_id=peer, device_id_type=MESH)

    copies = []

    def send(src, dst, where):
        k = len(copies)
        copy = pltpu.make_async_remote_copy(
            src_ref=src, dst_ref=dst, send_sem=send_sem.at[k], recv_sem=recv_sem.at[k],
            device_id=where, device_id_type=MESH,
        )
        copy.start()
        copies.append(copy)
        return copy

    first_row = (c * (NY * NZ) + f) * ROWS
    ends = jnp.concatenate([start_ref[...] - first_row, end_ref[...] - first_row], axis=0).T
    for k in range(4):
        scol[2 * k:2 * k + 2] = ends[:, k:k + 1].reshape(2, NY, KB, 1)
        ecol[2 * k:2 * k + 2] = ends[:, k + 4:k + 5].reshape(2, NY, KB, 1)

    forward = lambda s: s in (0, -1, -2, -3)
    via = lambda s: yb if forward(s) else ya
    other = lambda s: ya if forward(s) else yb
    slot = {s: i for i, s in enumerate(OFFS)}
    waits = {}

    def member_sums(pair):
        low, high = [], []
        for s in pair:
            for yy in (y, other(s), via(s), yc):
                low.append(scol[zat(s), yy])
                high.append(ecol[zat(s), yy])
        low = jnp.concatenate(low, axis=0)
        high = jnp.concatenate(high, axis=0)
        place = lax.broadcasted_iota(jnp.int32, (128, ROWS), 1)
        member = jnp.where((place >= low) & (place < high), 1.0, 0.0).astype(BF)
        sums = dot(member, tok[...]).astype(BF)
        for i, s in enumerate(pair):
            part[slot[s]] = sums[i * 64:(i + 1) * 64].reshape(NY, KB, D)

    def spread(pair):
        for s in pair:
            k = slot[s]
            waits["c", s] = send(part.at[k, 3], rc.at[k], at_y(via(s)))
            waits["d", s] = send(part.at[k, 2], rd.at[k], at_y(via(s)))

    def pass_on(pair):
        for s in pair:
            k = slot[s]
            waits["c", s].wait_recv()
            relay[k] = (part[k, 1].astype(F32) + rc[k].astype(F32)).astype(BF)
            waits["e", s] = send(relay.at[k], re.at[k], at_y(other(s)))

    def settle(pair):
        for s in pair:
            k = slot[s]
            waits["d", s].wait_recv()
            waits["e", s].wait_recv()
            done = part[k, 0].astype(F32) + rd[k].astype(F32) + re[k].astype(F32)
            if s == 0:
                return done
            red[k] = done.astype(BF)
            waits["z", s] = send(red.at[k], rz.at[k], at_z(zat(s)))

    def project(j, carry):
        cols = pl.ds(pl.multiple_of(j * 256, 256), 256)
        qkv[:, cols] = dot(tok[...], wqkv[:, cols]).astype(BF)
        return carry

    def local(it, carry):
        rows = pl.ds(pl.multiple_of((it // HEADS) * QB, QB), QB)
        col = (it % HEADS) * HS
        cols = pl.ds(pl.multiple_of(col, HS), HS)
        keys = qkv[:, pl.ds(pl.multiple_of(col + D, HS), HS)]
        vals = qkv[:, pl.ds(pl.multiple_of(col + 2 * D, HS), HS)]
        s = dot_nt(qkv[rows, cols], keys)
        m = jnp.max(s, axis=1, keepdims=True)
        p = jnp.exp2((s - m) * SCALE2)
        lloc[it] = jnp.sum(p, axis=1, keepdims=True)
        mloc[it] = m
        acc[rows, cols] = dot(p.astype(BF), vals)
        return carry

    projects = lambda a, b: lax.fori_loop(a, b, project, 0)
    locals_ = lambda a, b: lax.fori_loop(a, b, local, 0)

    p0, p1, p2, p3 = (4, 3), (-3, 2), (-2, 1), (-1, 0)
    loads[0].wait()
    member_sums(p0)
    pl.semaphore_wait(barrier, len(peers))
    spread(p0)
    for pair in (p1, p2, p3):
        member_sums(pair)
        spread(pair)
    pass_on(p0)
    loads[1].wait()
    projects(0, 1)
    pass_on(p1)
    projects(1, 2)
    settle(p0)
    pass_on(p2)
    settle(p1)
    projects(2, 4)
    pass_on(p3)
    settle(p2)
    projects(4, 6)
    total = settle(p3)
    projects(6, 10)
    for s in OFFS[1:]:
        waits["z", s].wait_recv()
        total = total + rz[slot[s]].astype(F32)
    span = (ecol[z, y] - scol[z, y]).astype(F32)
    pooled = (total / jnp.sqrt(span)).astype(BF)
    t1[4 + z, y] = pooled

    def gather(table, base, halo, work):
        near, turn, hops, outs = {}, {}, {}, []

        def over(zb, yy):
            src = table.at[base + zb, yy]
            if halo:
                half = zb // 4
                spot = half * (zb - 4) + (1 - half) * (zb + 12)
                outs.append(send(src, table.at[spot, yy], at_c((c + 2 * half + NC - 1) % NC)))
            else:
                outs.append(send(src, table.at[zb, yy], at_c(up)))
                outs.append(send(src, table.at[zb + 16, yy], at_c(down)))

        def alike(zb, yy, where):
            return send(table.at[base + zb, yy], table.at[base + zb, yy], where)

        for s in OFFS[1:]:
            hops[-s if s != 4 else 4] = alike(z, y, at_z(zat(s)))
        for i in range(len(OFFS) + 4):
            if i < 8:
                s = OFFS[i]
                zb = zat(s)
                if s != 0:
                    hops[s].wait_recv()
                near[s] = (alike(zb, y, at_y(ya)), alike(zb, y, at_y(yb)))
                over(zb, y)
            if 2 <= i < 10:
                s = OFFS[i - 2]
                zb = zat(s)
                first, second = near[s]
                first.wait_recv()
                if forward(s):
                    turn[s] = alike(zb, ya, at_y(yb))
                over(zb, ya)
                second.wait_recv()
                if not forward(s):
                    turn[s] = alike(zb, yb, at_y(ya))
                over(zb, yb)
            if i >= 4:
                s = OFFS[i - 4]
                turn[s].wait_recv()
                over(zat(s), yc)
            if i in work:
                work[i]()
        for copy in outs:
            copy.wait_recv()

    def absorb():
        query = dot(pooled, wqkv[:, 0:D]).astype(BF)
        for h in range(HEADS):
            qk[h * KB:(h + 1) * KB] = dot_nt(
                query[:, h * HS:(h + 1) * HS], wqkv[:, D + h * HS:D + (h + 1) * HS]
            ).astype(BF)

    gather(
        t1, 4, True,
        {
            0: absorb,
            2: lambda: projects(10, 12),
            4: lambda: locals_(0, 2),
            7: lambda: locals_(2, 4),
            9: lambda: locals_(4, 6),
            11: lambda: locals_(6, 8),
        },
    )

    table = t1[...].reshape(1024, D)
    s = dot_nt(qk[...], table)
    row = lax.broadcasted_iota(jnp.int32, s.shape, 0) % KB + f * KB
    key = lax.broadcasted_iota(jnp.int32, s.shape, 1) - REACH
    s = jnp.where(jnp.abs(row - key) <= REACH, s, -1e30)
    m = jnp.max(s, axis=1, keepdims=True)
    p = jnp.exp2((s - m) * SCALE2)
    w = (p / jnp.sum(p, axis=1, keepdims=True)).astype(BF)
    mixed = dot(w, table).astype(BF)
    mix = jnp.concatenate(
        [
            dot(mixed[h * KB:(h + 1) * KB], wqkv[:, 2 * D + h * HS:2 * D + (h + 1) * HS])
            for h in range(HEADS)
        ],
        axis=1,
    ).astype(BF)
    loads[2].wait()
    state = normalize(dot(mix, wco[...])).astype(BF)
    t2[8 + z, y] = state
    gather(
        t2, 8, False,
        {
            1: lambda: locals_(8, 10),
            5: lambda: locals_(10, 12),
            9: lambda: locals_(12, 14),
            11: lambda: locals_(14, 16),
        },
    )

    for n in range(2):
        for j in range(8):
            rel = jnp.minimum((list_ref[n, j] - (c - 1) * 32 + 512) % 256, 95)
            k = n * 8 + j
            gath[k * KB:(k + 1) * KB] = t2[rel // NY, rel % NY]
    loads[3].wait()

    def second(j, carry):
        cols = pl.ds(pl.multiple_of(j * 256, 256), 256)
        kv2[:, cols] = dot(gath[...], wkv2[:, cols]).astype(BF)
        return carry

    lax.fori_loop(0, 8, second, 0)

    def remote(it, carry):
        n = it // HEADS
        rows = pl.ds(pl.multiple_of(n * QB, QB), QB)
        col = (it % HEADS) * HS
        cols = pl.ds(pl.multiple_of(col, HS), HS)
        listed = pl.ds(pl.multiple_of(n * 128, 128), 128)
        s = dot_nt(qkv[rows, cols], kv2[listed, cols])
        m0 = mloc[it]
        m = jnp.maximum(m0, jnp.max(s, axis=1, keepdims=True))
        a = jnp.exp2((m0 - m) * SCALE2)
        p = jnp.exp2((s - m) * SCALE2)
        total = a * lloc[it] + jnp.sum(p, axis=1, keepdims=True)
        vals = kv2[listed, pl.ds(pl.multiple_of(col + D, HS), HS)]
        o = acc[rows, cols] * a + dot(p.astype(BF), vals)
        att[rows, cols] = (o / total).astype(BF)
        return carry

    lax.fori_loop(0, 16, remote, 0, unroll=2)
    for copy in copies:
        copy.wait_send()


def body(tokens, w_qkv, w_coarse_out, w_kv2, w_out, seg_start, seg_end, block_lists):
    vmem = lambda shape, kind: pltpu.VMEM(shape, kind)
    attended = pl.pallas_call(
        kernel,
        out_shape=jax.ShapeDtypeStruct((ROWS, D), BF),
        in_specs=[
            pl.BlockSpec(memory_space=pltpu.VMEM),
            pl.BlockSpec(memory_space=pltpu.VMEM),
            pl.BlockSpec(memory_space=pltpu.SMEM),
        ] + [pl.BlockSpec(memory_space=pltpu.HBM)] * 4,
        out_specs=pl.BlockSpec(memory_space=pltpu.VMEM),
        scratch_shapes=[
            vmem((ROWS, D), BF),
            vmem((D, 3 * D), BF),
            vmem((D, D), BF),
            vmem((D, 2 * D), BF),
            vmem((NZ, NY, KB, 1), jnp.int32),
            vmem((NZ, NY, KB, 1), jnp.int32),
            vmem((NZ, NY, KB, D), BF),
            vmem((NZ, KB, D), BF),
            vmem((NZ, KB, D), BF),
            vmem((NZ, KB, D), BF),
            vmem((NZ, KB, D), BF),
            vmem((NZ, KB, D), BF),
            vmem((NZ, KB, D), BF),
            vmem((16, NY, KB, D), BF),
            vmem((24, NY, KB, D), BF),
            vmem((ROWS, 3 * D), BF),
            vmem((ROWS, D), F32),
            vmem((16, QB, 1), F32),
            vmem((16, QB, 1), F32),
            vmem((HEADS * KB, D), BF),
            vmem((256, D), BF),
            vmem((256, 2 * D), BF),
            pltpu.SemaphoreType.DMA((4,)),
            pltpu.SemaphoreType.DMA((COPIES,)),
            pltpu.SemaphoreType.DMA((COPIES,)),
        ],
        compiler_params=pltpu.CompilerParams(
            collective_id=0, has_side_effects=True, vmem_limit_bytes=60 * 1024 * 1024
        ),
    )(
        seg_start.reshape(4, 128), seg_end.reshape(4, 128), block_lists,
        tokens, w_qkv, w_coarse_out, w_kv2,
    )
    return normalize(dot(attended, w_out)).astype(BF)


def solution(mesh):
    placed = (
        P(("coarse", "fine"), None),
        P(),
        P(),
        P(),
        P(),
        P("coarse"),
        P("coarse"),
        P(("coarse", "fine"), None),
    )
    return jax.shard_map(
        body, mesh=mesh, in_specs=placed, out_specs=P(("coarse", "fine"), None), check_vma=False
    )
```

```python
import math

import jax
import jax.numpy as jnp
from jax import lax
from jax.experimental import pallas as pl
from jax.experimental.pallas import tpu as pltpu
from jax.sharding import PartitionSpec as P

HEADS = 8
KB = 16
QB = 256
NY = 4
NZ = 8
NC = 8
D = 1024
HS = 128
ROWS = 512
SEGS = 512
REACH = 256
SCALE = 1.0 / math.sqrt(HS)
SCALE2 = SCALE * math.log2(math.e)
BF = jnp.bfloat16
F32 = jnp.float32
NT = (((1,), (1,)), ((), ()))
MESH = pl.DeviceIdType.MESH


def dot(a, b):
    return jnp.dot(a, b, preferred_element_type=F32)


def dot_nt(a, b):
    return lax.dot_general(a, b, NT, preferred_element_type=F32)


def normalize(x):
    return x * lax.rsqrt(jnp.mean(x * x, axis=-1, keepdims=True) + 1e-06)


OFFS = (0, -1, 1, -2, 2, -3, 3, 4)
COPIES = 31 + 24 + 95


def kernel(
    start_ref, end_ref, list_ref, tok_hbm, wqkv_hbm, wco_hbm, wkv2_hbm, wout_hbm,
    out_ref, tok, wqkv, wco, wkv2, wout, scol, ecol, part, rc, rd, re, relay, red, rz, t1, tq, po, pm, go, gm, t2, qkv, acc,
    mloc, lloc, qk, gath, kv2, att, load_sem, send_sem, recv_sem,
):
    c = lax.axis_index("coarse")
    f = lax.axis_index("fine")
    z = f // NY
    y = f % NY
    ya = y + 1 - 2 * (y % 2)
    yb = 3 - y
    yc = (y + 2) % 4
    up = (c + 1) % NC
    down = (c + NC - 1) % NC

    loads = [
        pltpu.make_async_copy(src, dst, load_sem.at[i])
        for i, (src, dst) in enumerate(
            ((tok_hbm, tok), (wqkv_hbm, wqkv), (wco_hbm, wco), (wkv2_hbm, wkv2), (wout_hbm, wout))
        )
    ]
    for load in loads:
        load.start()

    at_y = lambda yy: {"fine": z * NY + yy}
    at_z = lambda zz: {"fine": zz * NY + y}
    at_c = lambda cc: {"coarse": cc}
    zat = lambda s: (z + s + NZ) % NZ

    barrier = pltpu.get_barrier_semaphore()
    peers = [at_z(zat(s)) for s in OFFS[1:]]
    peers += [at_y(ya), at_y(yb), at_y(yc), at_c(up), at_c(down)]
    for peer in peers:
        pl.semaphore_signal(barrier, inc=1, device_id=peer, device_id_type=MESH)

    copies = []

    def send(src, dst, where):
        k = len(copies)
        copy = pltpu.make_async_remote_copy(
            src_ref=src, dst_ref=dst, send_sem=send_sem.at[k], recv_sem=recv_sem.at[k],
            device_id=where, device_id_type=MESH,
        )
        copy.start()
        copies.append(copy)
        return copy

    first_row = (c * (NY * NZ) + f) * ROWS
    ends = jnp.concatenate([start_ref[...] - first_row, end_ref[...] - first_row], axis=0).T
    for k in range(4):
        scol[2 * k:2 * k + 2] = ends[:, k:k + 1].reshape(2, NY, KB, 1)
        ecol[2 * k:2 * k + 2] = ends[:, k + 4:k + 5].reshape(2, NY, KB, 1)

    forward = lambda s: s in (0, -1, -2, -3)
    via = lambda s: yb if forward(s) else ya
    other = lambda s: ya if forward(s) else yb
    slot = {s: i for i, s in enumerate(OFFS)}
    waits = {}

    def member_sums(pair):
        low, high = [], []
        for s in pair:
            for yy in (y, other(s), via(s), yc):
                low.append(scol[zat(s), yy])
                high.append(ecol[zat(s), yy])
        low = jnp.concatenate(low, axis=0)
        high = jnp.concatenate(high, axis=0)
        place = lax.broadcasted_iota(jnp.int32, (128, ROWS), 1)
        member = jnp.where((place >= low) & (place < high), 1.0, 0.0).astype(BF)
        sums = dot(member, tok[...]).astype(BF)
        for i, s in enumerate(pair):
            part[slot[s]] = sums[i * 64:(i + 1) * 64].reshape(NY, KB, D)

    def spread(pair):
        for s in pair:
            k = slot[s]
            waits["c", s] = send(part.at[k, 3], rc.at[k], at_y(via(s)))

    def pass_on(pair):
        for s in pair:
            k = slot[s]
            waits["c", s].wait_recv()
            relay[k] = (part[k, 1].astype(F32) + rc[k].astype(F32)).astype(BF)
            waits["e", s] = send(relay.at[k], re.at[k], at_y(other(s)))
        for s in pair:
            k = slot[s]
            waits["d", s] = send(part.at[k, 2], rd.at[k], at_y(via(s)))

    def settle(pair):
        for s in pair:
            k = slot[s]
            waits["d", s].wait_recv()
            waits["e", s].wait_recv()
            done = part[k, 0].astype(F32) + rd[k].astype(F32) + re[k].astype(F32)
            if s == 0:
                return done
            red[k] = done.astype(BF)
            waits["z", s] = send(red.at[k], rz.at[k], at_z(zat(s)))

    def project(j, carry):
        cols = pl.ds(pl.multiple_of(j * 256, 256), 256)
        qkv[:, cols] = dot(tok[...], wqkv[:, cols]).astype(BF)
        return carry

    def local(it, carry):
        rows = pl.ds(pl.multiple_of((it // HEADS) * QB, QB), QB)
        col = (it % HEADS) * HS
        cols = pl.ds(pl.multiple_of(col, HS), HS)
        keys = qkv[:, pl.ds(pl.multiple_of(col + D, HS), HS)]
        vals = qkv[:, pl.ds(pl.multiple_of(col + 2 * D, HS), HS)]
        s = dot_nt(qkv[rows, cols], keys)
        m = jnp.max(s, axis=1, keepdims=True)
        p = jnp.exp2((s - m) * SCALE2)
        lloc[it] = jnp.sum(p, axis=1, keepdims=True)
        mloc[it] = m
        acc[rows, cols] = dot(p.astype(BF), vals)
        return carry

    projects = lambda a, b: lax.fori_loop(a, b, project, 0)
    locals_ = lambda a, b: lax.fori_loop(a, b, local, 0)

    pairs = (4, 3), (-3, 2), (-2, 1), (-1, 0)
    loads[0].wait()
    for pair in pairs:
        member_sums(pair)
    pl.semaphore_wait(barrier, len(peers))
    for pair in pairs:
        spread(pair)
    loads[1].wait()
    projects(0, 3)
    pass_on(pairs[0])
    pass_on(pairs[1])
    projects(3, 4)
    settle(pairs[0])
    pass_on(pairs[2])
    projects(4, 5)
    settle(pairs[1])
    pass_on(pairs[3])
    projects(5, 7)
    settle(pairs[2])
    projects(7, 9)
    total = settle(pairs[3])
    projects(9, 12)
    for s in OFFS[1:]:
        waits["z", s].wait_recv()
        total = total + rz[slot[s]].astype(F32)
    span = (ecol[z, y] - scol[z, y]).astype(F32)
    pooled = (total / jnp.sqrt(span)).astype(BF)
    t1[4 + z] = pooled
    tq[y] = pooled

    def across(zb):
        half = zb // 4
        spot = half * (zb - 4) + (1 - half) * (zb + 12)
        return send(t1.at[4 + zb], t1.at[spot], at_c((c + 2 * half + NC - 1) % NC))

    hops = {}
    rows_in = []
    for s in (1, -1, 4, 3, -3, 2, -2):
        hops[-s if s != 4 else 4] = send(t1.at[4 + z], t1.at[4 + z], at_z(zat(s)))
    for yy in (yc, ya, yb):
        rows_in.append(send(tq.at[y], tq.at[y], at_y(yy)))
    halo = [across(z)]
    for copy in rows_in:
        copy.wait_recv()

    query = dot(tq[...].reshape(64, D), wqkv[:, 0:D]).astype(BF)

    def absorb(h):
        qk[h * 64:(h + 1) * 64] = dot_nt(
            query[:, h * HS:(h + 1) * HS], wqkv[:, D + h * HS:D + (h + 1) * HS]
        ).astype(BF)

    absorb(0)
    absorb(1)
    for i, s in enumerate((-1, 1, -2, 2, -3, 3, 4)):
        hops[s].wait_recv()
        halo.append(across(zat(s)))
        if i < 6:
            absorb(2 + i)
    locals_(0, 5)
    for copy in halo:
        copy.wait_recv()

    table = t1[...].reshape(256, D)
    s = dot_nt(qk[...], table)
    row = z * 64 + lax.broadcasted_iota(jnp.int32, s.shape, 0) % 64
    place = lax.broadcasted_iota(jnp.int32, s.shape, 1)
    key = place // KB * 64 + place % KB + y * KB - REACH
    s = jnp.where(jnp.abs(row - key) <= REACH, s, -1e30)
    m = jnp.max(s, axis=1, keepdims=True)
    p = jnp.exp2((s - m) * SCALE2)
    l = jnp.sum(p, axis=1, keepdims=True)
    mixed = dot(p.astype(BF), table).astype(BF)
    lane = lax.broadcasted_iota(jnp.int32, (64, HS), 1)
    tops = jnp.zeros((64, HS), F32)
    sums = jnp.ones((64, HS), F32)
    for h in range(HEADS):
        rows = slice(h * 64, (h + 1) * 64)
        tops = jnp.where(lane == h, m[rows], tops)
        sums = jnp.where(lane == h, l[rows], sums)
        cols = slice(2 * D + h * HS, 2 * D + (h + 1) * HS)
        po[:, :, h * HS:(h + 1) * HS] = dot(mixed[rows], wqkv[:, cols]).astype(BF).reshape(
            NY, KB, HS
        )
    pm[:, 0] = tops.reshape(NY, KB, HS)
    pm[:, 1] = sums.reshape(NY, KB, HS)
    parts = []
    for j, yy in enumerate((yc, ya, yb)):
        parts.append(send(pm.at[yy], gm.at[j], at_y(yy)))
        parts.append(send(po.at[yy], go.at[j], at_y(yy)))
    locals_(5, 7)
    for copy in parts:
        copy.wait_recv()
    tops = [pm[y, 0]] + [gm[j, 0] for j in range(3)]
    sums = [pm[y, 1]] + [gm[j, 1] for j in range(3)]
    outs = [po[y].astype(F32)] + [go[j].astype(F32) for j in range(3)]
    peak = jnp.maximum(jnp.maximum(tops[0], tops[1]), jnp.maximum(tops[2], tops[3]))
    shares = [jnp.exp2((t - peak) * SCALE2) for t in tops]
    whole = sum(a * b for a, b in zip(shares, sums))
    shares = [a / whole for a in shares]
    mix = jnp.concatenate(
        [
            sum(a[:, h:h + 1] * o[:, h * HS:(h + 1) * HS] for a, o in zip(shares, outs))
            for h in range(HEADS)
        ],
        axis=1,
    ).astype(BF)
    loads[2].wait()
    state = normalize(dot(mix, wco[...])).astype(BF)
    t2[8 + z, y] = state
    near, turn, hops, halo = {}, {}, {}, []

    def over(zb, yy):
        src = t2.at[8 + zb, yy]
        halo.append(send(src, t2.at[zb, yy], at_c(up)))
        halo.append(send(src, t2.at[zb + 16, yy], at_c(down)))

    def alike(zb, yy, where):
        return send(t2.at[8 + zb, yy], t2.at[8 + zb, yy], where)

    def event(kind, s):
        zb = zat(s)
        if kind == "z":
            if s != 0:
                hops[s].wait_recv()
            near[s] = (alike(zb, y, at_y(ya)), alike(zb, y, at_y(yb)))
            over(zb, y)
        elif kind == "y":
            first, second = near[s]
            first.wait_recv()
            if forward(s):
                turn[s] = alike(zb, ya, at_y(yb))
            second.wait_recv()
            if not forward(s):
                turn[s] = alike(zb, yb, at_y(ya))
            over(zb, ya)
            over(zb, yb)
        elif kind == "c":
            turn[s].wait_recv()
            over(zb, yc)
        else:
            locals_(s, s + 1)

    for s in (1, -1, 4, 3, -3, 2, -2):
        hops[-s if s != 4 else 4] = alike(z, y, at_z(zat(s)))
    for kind, s in (
        ("z", 0), ("w", 7), ("w", 8), ("w", 9), ("w", 10), ("y", 0), ("z", -1), ("z", 1),
        ("w", 11), ("z", -2), ("z", 2), ("w", 12), ("c", 0), ("z", -3), ("z", 3), ("z", 4),
        ("y", -1), ("y", 1), ("w", 13), ("y", -2), ("y", 2), ("c", -1), ("c", 1), ("y", -3),
        ("y", 3), ("w", 14), ("c", -2), ("c", 2), ("y", 4), ("c", -3), ("c", 3), ("w", 15),
        ("c", 4),
    ):
        event(kind, s)
    for copy in halo:
        copy.wait_recv()

    for n in range(2):
        for j in range(8):
            rel = jnp.minimum((list_ref[n, j] - (c - 1) * 32 + 512) % 256, 95)
            k = n * 8 + j
            gath[k * KB:(k + 1) * KB] = t2[rel // NY, rel % NY]
    loads[3].wait()

    def second(j, carry):
        cols = pl.ds(pl.multiple_of(j * 256, 256), 256)
        kv2[:, cols] = dot(gath[...], wkv2[:, cols]).astype(BF)
        return carry

    lax.fori_loop(0, 8, second, 0)

    def remote(it, carry):
        n = it // HEADS
        rows = pl.ds(pl.multiple_of(n * QB, QB), QB)
        col = (it % HEADS) * HS
        cols = pl.ds(pl.multiple_of(col, HS), HS)
        listed = pl.ds(pl.multiple_of(n * 128, 128), 128)
        s = dot_nt(qkv[rows, cols], kv2[listed, cols])
        m0 = mloc[it]
        m = jnp.maximum(m0, jnp.max(s, axis=1, keepdims=True))
        a = jnp.exp2((m0 - m) * SCALE2)
        p = jnp.exp2((s - m) * SCALE2)
        total = a * lloc[it] + jnp.sum(p, axis=1, keepdims=True)
        vals = kv2[listed, pl.ds(pl.multiple_of(col + D, HS), HS)]
        o = acc[rows, cols] * a + dot(p.astype(BF), vals)
        att[rows, cols] = (o / total).astype(BF)
        return carry

    lax.fori_loop(0, 16, remote, 0, unroll=4)
    loads[4].wait()

    def finish(i, carry):
        rows = pl.ds(pl.multiple_of(i * 128, 128), 128)
        out_ref[rows, :] = normalize(dot(att[rows, :], wout[...])).astype(BF)
        return carry

    lax.fori_loop(0, 4, finish, 0)
    for copy in copies:
        copy.wait_send()


def body(tokens, w_qkv, w_coarse_out, w_kv2, w_out, seg_start, seg_end, block_lists):
    vmem = lambda shape, kind: pltpu.VMEM(shape, kind)
    return pl.pallas_call(
        kernel,
        out_shape=jax.ShapeDtypeStruct((ROWS, D), BF),
        in_specs=[
            pl.BlockSpec(memory_space=pltpu.VMEM),
            pl.BlockSpec(memory_space=pltpu.VMEM),
            pl.BlockSpec(memory_space=pltpu.SMEM),
        ] + [pl.BlockSpec(memory_space=pltpu.HBM)] * 5,
        out_specs=pl.BlockSpec(memory_space=pltpu.VMEM),
        scratch_shapes=[
            vmem((ROWS, D), BF),
            vmem((D, 3 * D), BF),
            vmem((D, D), BF),
            vmem((D, 2 * D), BF),
            vmem((D, D), BF),
            vmem((NZ, NY, KB, 1), jnp.int32),
            vmem((NZ, NY, KB, 1), jnp.int32),
            vmem((NZ, NY, KB, D), BF),
            vmem((NZ, KB, D), BF),
            vmem((NZ, KB, D), BF),
            vmem((NZ, KB, D), BF),
            vmem((NZ, KB, D), BF),
            vmem((NZ, KB, D), BF),
            vmem((NZ, KB, D), BF),
            vmem((16, KB, D), BF),
            vmem((NY, KB, D), BF),
            vmem((NY, KB, D), BF),
            vmem((NY, 2, KB, HS), F32),
            vmem((3, KB, D), BF),
            vmem((3, 2, KB, HS), F32),
            vmem((24, NY, KB, D), BF),
            vmem((ROWS, 3 * D), BF),
            vmem((ROWS, D), F32),
            vmem((16, QB, 1), F32),
            vmem((16, QB, 1), F32),
            vmem((HEADS * 64, D), BF),
            vmem((256, D), BF),
            vmem((256, 2 * D), BF),
            vmem((ROWS, D), BF),
            pltpu.SemaphoreType.DMA((5,)),
            pltpu.SemaphoreType.DMA((COPIES,)),
            pltpu.SemaphoreType.DMA((COPIES,)),
        ],
        compiler_params=pltpu.CompilerParams(
            collective_id=0, has_side_effects=True, vmem_limit_bytes=54 * 1024 * 1024
        ),
    )(
        seg_start.reshape(4, 128), seg_end.reshape(4, 128), block_lists,
        tokens, w_qkv, w_coarse_out, w_kv2, w_out,
    )


def solution(mesh):
    placed = (
        P(("coarse", "fine"), None),
        P(),
        P(),
        P(),
        P(),
        P("coarse"),
        P("coarse"),
        P(("coarse", "fine"), None),
    )
    return jax.shard_map(
        body, mesh=mesh, in_specs=placed, out_specs=P(("coarse", "fine"), None), check_vma=False
    )
```

```python
import math

import jax
import jax.numpy as jnp
from jax import lax
from jax.experimental import pallas as pl
from jax.experimental.pallas import tpu as pltpu
from jax.sharding import PartitionSpec as P

HEADS = 8
KB = 16
QB = 256
NY = 4
NZ = 8
NC = 8
D = 1024
HS = 128
ROWS = 512
SEGS = 512
REACH = 256
SCALE = 1.0 / math.sqrt(HS)
SCALE2 = SCALE * math.log2(math.e)
BF = jnp.bfloat16
F32 = jnp.float32
NT = (((1,), (1,)), ((), ()))
MESH = pl.DeviceIdType.MESH


def dot(a, b):
    return jnp.dot(a, b, preferred_element_type=F32)


def dot_nt(a, b):
    return lax.dot_general(a, b, NT, preferred_element_type=F32)


def normalize(x):
    return x * lax.rsqrt(jnp.mean(x * x, axis=-1, keepdims=True) + 1e-06)


OFFS = (0, -1, 1, -2, 2, -3, 3, 4)
COPIES = 31 + 24 + 95


def kernel(
    start_ref, end_ref, list_ref, tok_hbm, wqkv_hbm, wco_hbm, wkv2_hbm, wout_hbm,
    out_ref, tok, wqkv, wco, wkv2, wout, scol, ecol, part, rc, rd, re, relay, red, rz, t1, tq, po, pm, go, gm, t2, qkv, acc,
    mloc, lloc, qk, gath, kv2, att, load_sem, send_sem, recv_sem,
):
    c = lax.axis_index("coarse")
    f = lax.axis_index("fine")
    z = f // NY
    y = f % NY
    ya = y + 1 - 2 * (y % 2)
    yb = 3 - y
    yc = (y + 2) % 4
    up = (c + 1) % NC
    down = (c + NC - 1) % NC

    loads = [
        pltpu.make_async_copy(src, dst, load_sem.at[i])
        for i, (src, dst) in enumerate(
            ((tok_hbm, tok), (wqkv_hbm, wqkv), (wco_hbm, wco), (wkv2_hbm, wkv2), (wout_hbm, wout))
        )
    ]
    loads[0].start()

    at_y = lambda yy: {"fine": z * NY + yy}
    at_z = lambda zz: {"fine": zz * NY + y}
    at_c = lambda cc: {"coarse": cc}
    zat = lambda s: (z + s + NZ) % NZ

    barrier = pltpu.get_barrier_semaphore()
    peers = [at_z(zat(s)) for s in OFFS[1:]]
    peers += [at_y(ya), at_y(yb), at_y(yc), at_c(up), at_c(down)]
    for peer in peers:
        pl.semaphore_signal(barrier, inc=1, device_id=peer, device_id_type=MESH)

    copies = []

    def send(src, dst, where):
        k = len(copies)
        copy = pltpu.make_async_remote_copy(
            src_ref=src, dst_ref=dst, send_sem=send_sem.at[k], recv_sem=recv_sem.at[k],
            device_id=where, device_id_type=MESH,
        )
        copy.start()
        copies.append(copy)
        return copy

    first_row = (c * (NY * NZ) + f) * ROWS
    ends = jnp.concatenate([start_ref[...] - first_row, end_ref[...] - first_row], axis=0).T
    for k in range(4):
        scol[2 * k:2 * k + 2] = ends[:, k:k + 1].reshape(2, NY, KB, 1)
        ecol[2 * k:2 * k + 2] = ends[:, k + 4:k + 5].reshape(2, NY, KB, 1)

    forward = lambda s: s in (0, -1, -2, -3)
    via = lambda s: yb if forward(s) else ya
    other = lambda s: ya if forward(s) else yb
    slot = {s: i for i, s in enumerate(OFFS)}
    waits = {}

    def member_sums(pair):
        low, high = [], []
        for s in pair:
            for yy in (y, other(s), via(s), yc):
                low.append(scol[zat(s), yy])
                high.append(ecol[zat(s), yy])
        low = jnp.concatenate(low, axis=0)
        high = jnp.concatenate(high, axis=0)
        place = lax.broadcasted_iota(jnp.int32, (128, ROWS), 1)
        member = jnp.where((place >= low) & (place < high), 1.0, 0.0).astype(BF)
        sums = dot(member, tok[...]).astype(BF)
        for i, s in enumerate(pair):
            part[slot[s]] = sums[i * 64:(i + 1) * 64].reshape(NY, KB, D)

    def spread(pair):
        for s in pair:
            k = slot[s]
            waits["c", s] = send(part.at[k, 3], rc.at[k], at_y(via(s)))

    def pass_on(pair):
        for s in pair:
            k = slot[s]
            waits["c", s].wait_recv()
            relay[k] = (part[k, 1].astype(F32) + rc[k].astype(F32)).astype(BF)
            waits["e", s] = send(relay.at[k], re.at[k], at_y(other(s)))
        for s in pair:
            k = slot[s]
            waits["d", s] = send(part.at[k, 2], rd.at[k], at_y(via(s)))

    def settle(pair):
        for s in pair:
            k = slot[s]
            waits["d", s].wait_recv()
            waits["e", s].wait_recv()
            done = part[k, 0].astype(F32) + rd[k].astype(F32) + re[k].astype(F32)
            if s == 0:
                return done
            red[k] = done.astype(BF)
            waits["z", s] = send(red.at[k], rz.at[k], at_z(zat(s)))

    def project(j, carry):
        cols = pl.ds(pl.multiple_of(j * 256, 256), 256)
        qkv[:, cols] = dot(tok[...], wqkv[:, cols]).astype(BF)
        return carry

    def local(it, carry):
        rows = pl.ds(pl.multiple_of((it // HEADS) * QB, QB), QB)
        col = (it % HEADS) * HS
        cols = pl.ds(pl.multiple_of(col, HS), HS)
        keys = qkv[:, pl.ds(pl.multiple_of(col + D, HS), HS)]
        vals = qkv[:, pl.ds(pl.multiple_of(col + 2 * D, HS), HS)]
        s = dot_nt(qkv[rows, cols], keys)
        m = jnp.max(s, axis=1, keepdims=True)
        p = jnp.exp2((s - m) * SCALE2)
        lloc[it] = jnp.broadcast_to(jnp.sum(p, axis=1, keepdims=True), (QB, HS))
        mloc[it] = jnp.broadcast_to(m, (QB, HS))
        acc[rows, cols] = dot(p.astype(BF), vals)
        return carry

    projects = lambda a, b: lax.fori_loop(a, b, project, 0)
    locals_ = lambda a, b: lax.fori_loop(a, b, local, 0)

    pairs = (4, 3), (-3, 2), (-2, 1), (-1, 0)
    loads[0].wait()
    for load in loads[1:]:
        load.start()
    for pair in pairs:
        member_sums(pair)
    pl.semaphore_wait(barrier, len(peers))
    for pair in pairs:
        spread(pair)
    loads[1].wait()
    projects(0, 3)
    pass_on(pairs[0])
    pass_on(pairs[1])
    projects(3, 4)
    settle(pairs[0])
    pass_on(pairs[2])
    projects(4, 5)
    settle(pairs[1])
    pass_on(pairs[3])
    projects(5, 7)
    settle(pairs[2])
    projects(7, 9)
    total = settle(pairs[3])
    projects(9, 12)
    for s in OFFS[1:]:
        waits["z", s].wait_recv()
        total = total + rz[slot[s]].astype(F32)
    span = (ecol[z, y] - scol[z, y]).astype(F32)
    pooled = (total / jnp.sqrt(span)).astype(BF)
    t1[4 + z] = pooled
    tq[y] = pooled

    def across(zb):
        half = zb // 4
        spot = half * (zb - 4) + (1 - half) * (zb + 12)
        return send(t1.at[4 + zb], t1.at[spot], at_c((c + 2 * half + NC - 1) % NC))

    hops = {}
    rows_in = []
    for s in (1, -1, 4, 3, -3, 2, -2):
        hops[-s if s != 4 else 4] = send(t1.at[4 + z], t1.at[4 + z], at_z(zat(s)))
    for yy in (yc, ya, yb):
        rows_in.append(send(tq.at[y], tq.at[y], at_y(yy)))
    halo = [across(z)]
    for copy in rows_in:
        copy.wait_recv()

    query = dot(tq[...].reshape(64, D), wqkv[:, 0:D]).astype(BF)

    def absorb(h):
        qk[h * 64:(h + 1) * 64] = dot_nt(
            query[:, h * HS:(h + 1) * HS], wqkv[:, D + h * HS:D + (h + 1) * HS]
        ).astype(BF)

    absorb(0)
    absorb(1)
    for i, s in enumerate((-1, 1, -2, 2, -3, 3, 4)):
        hops[s].wait_recv()
        halo.append(across(zat(s)))
        if i < 6:
            absorb(2 + i)
    locals_(0, 5)
    for copy in halo:
        copy.wait_recv()

    table = t1[...].reshape(256, D)
    s = dot_nt(qk[...], table)
    row = z * 64 + lax.broadcasted_iota(jnp.int32, s.shape, 0) % 64
    place = lax.broadcasted_iota(jnp.int32, s.shape, 1)
    key = place // KB * 64 + place % KB + y * KB - REACH
    s = jnp.where(jnp.abs(row - key) <= REACH, s, -1e30)
    m = jnp.max(s, axis=1, keepdims=True)
    p = jnp.exp2((s - m) * SCALE2)
    l = jnp.sum(p, axis=1, keepdims=True)
    mixed = dot(p.astype(BF), table).astype(BF)
    lane = lax.broadcasted_iota(jnp.int32, (64, HS), 1)
    tops = jnp.zeros((64, HS), F32)
    sums = jnp.ones((64, HS), F32)
    for h in range(HEADS):
        rows = slice(h * 64, (h + 1) * 64)
        tops = jnp.where(lane == h, m[rows], tops)
        sums = jnp.where(lane == h, l[rows], sums)
        cols = slice(2 * D + h * HS, 2 * D + (h + 1) * HS)
        po[:, :, h * HS:(h + 1) * HS] = dot(mixed[rows], wqkv[:, cols]).astype(BF).reshape(
            NY, KB, HS
        )
    pm[:, 0] = tops.reshape(NY, KB, HS)
    pm[:, 1] = sums.reshape(NY, KB, HS)
    parts = []
    for j, yy in enumerate((yc, ya, yb)):
        parts.append(send(pm.at[yy], gm.at[j], at_y(yy)))
        parts.append(send(po.at[yy], go.at[j], at_y(yy)))
    locals_(5, 7)
    for copy in parts:
        copy.wait_recv()
    tops = [pm[y, 0]] + [gm[j, 0] for j in range(3)]
    sums = [pm[y, 1]] + [gm[j, 1] for j in range(3)]
    outs = [po[y].astype(F32)] + [go[j].astype(F32) for j in range(3)]
    peak = jnp.maximum(jnp.maximum(tops[0], tops[1]), jnp.maximum(tops[2], tops[3]))
    shares = [jnp.exp2((t - peak) * SCALE2) for t in tops]
    whole = sum(a * b for a, b in zip(shares, sums))
    shares = [a / whole for a in shares]
    mix = jnp.concatenate(
        [
            sum(a[:, h:h + 1] * o[:, h * HS:(h + 1) * HS] for a, o in zip(shares, outs))
            for h in range(HEADS)
        ],
        axis=1,
    ).astype(BF)
    loads[2].wait()
    state = normalize(dot(mix, wco[...])).astype(BF)
    t2[8 + z, y] = state
    near, turn, hops, halo = {}, {}, {}, []

    def over(zb, yy):
        src = t2.at[8 + zb, yy]
        halo.append(send(src, t2.at[zb, yy], at_c(up)))
        halo.append(send(src, t2.at[zb + 16, yy], at_c(down)))

    def alike(zb, yy, where):
        return send(t2.at[8 + zb, yy], t2.at[8 + zb, yy], where)

    def event(kind, s):
        zb = zat(s)
        if kind == "z":
            if s != 0:
                hops[s].wait_recv()
            near[s] = (alike(zb, y, at_y(ya)), alike(zb, y, at_y(yb)))
            over(zb, y)
        elif kind == "y":
            first, second = near[s]
            first.wait_recv()
            if forward(s):
                turn[s] = alike(zb, ya, at_y(yb))
            second.wait_recv()
            if not forward(s):
                turn[s] = alike(zb, yb, at_y(ya))
            over(zb, ya)
            over(zb, yb)
        elif kind == "c":
            turn[s].wait_recv()
            over(zb, yc)
        else:
            locals_(s, s + 1)

    for s in (1, -1, 4, 3, -3, 2, -2):
        hops[-s if s != 4 else 4] = alike(z, y, at_z(zat(s)))
    for kind, s in (
        ("z", 0), ("w", 7), ("w", 8), ("w", 9), ("w", 10), ("y", 0), ("z", -1), ("z", 1),
        ("w", 11), ("z", -2), ("z", 2), ("w", 12), ("c", 0), ("z", -3), ("z", 3), ("z", 4),
        ("y", -1), ("y", 1), ("w", 13), ("y", -2), ("y", 2), ("c", -1), ("c", 1), ("y", -3),
        ("y", 3), ("w", 14), ("c", -2), ("c", 2), ("y", 4), ("c", -3), ("c", 3), ("w", 15),
        ("c", 4),
    ):
        event(kind, s)
    for copy in halo:
        copy.wait_recv()

    for n in range(2):
        for j in range(8):
            rel = jnp.minimum((list_ref[n, j] - (c - 1) * 32 + 512) % 256, 95)
            k = n * 8 + j
            gath[k * KB:(k + 1) * KB] = t2[rel // NY, rel % NY]
    loads[3].wait()

    def second(j, carry):
        cols = pl.ds(pl.multiple_of(j * 256, 256), 256)
        kv2[:, cols] = dot(gath[...], wkv2[:, cols]).astype(BF)
        return carry

    lax.fori_loop(0, 8, second, 0)

    def remote(it, carry):
        n = it // HEADS
        rows = pl.ds(pl.multiple_of(n * QB, QB), QB)
        col = (it % HEADS) * HS
        cols = pl.ds(pl.multiple_of(col, HS), HS)
        listed = pl.ds(pl.multiple_of(n * 128, 128), 128)
        s = dot_nt(qkv[rows, cols], kv2[listed, cols])
        m0 = mloc[it]
        m = jnp.maximum(m0, jnp.max(s, axis=1, keepdims=True))
        a = jnp.exp2((m0 - m) * SCALE2)
        p = jnp.exp2((s - m) * SCALE2)
        total = a * lloc[it] + jnp.sum(p, axis=1, keepdims=True)
        vals = kv2[listed, pl.ds(pl.multiple_of(col + D, HS), HS)]
        o = acc[rows, cols] * a + dot(p.astype(BF), vals)
        att[rows, cols] = (o * (1.0 / total)).astype(BF)
        return carry

    lax.fori_loop(0, 16, remote, 0, unroll=8)
    loads[4].wait()

    def finish(i, carry):
        rows = pl.ds(pl.multiple_of(i * 256, 256), 256)
        out_ref[rows, :] = normalize(dot(att[rows, :], wout[...])).astype(BF)
        return carry

    lax.fori_loop(0, 2, finish, 0)
    for copy in copies:
        copy.wait_send()


def body(tokens, w_qkv, w_coarse_out, w_kv2, w_out, seg_start, seg_end, block_lists):
    vmem = lambda shape, kind: pltpu.VMEM(shape, kind)
    return pl.pallas_call(
        kernel,
        out_shape=jax.ShapeDtypeStruct((ROWS, D), BF),
        in_specs=[
            pl.BlockSpec(memory_space=pltpu.VMEM),
            pl.BlockSpec(memory_space=pltpu.VMEM),
            pl.BlockSpec(memory_space=pltpu.SMEM),
        ] + [pl.BlockSpec(memory_space=pltpu.HBM)] * 5,
        out_specs=pl.BlockSpec(memory_space=pltpu.VMEM),
        scratch_shapes=[
            vmem((ROWS, D), BF),
            vmem((D, 3 * D), BF),
            vmem((D, D), BF),
            vmem((D, 2 * D), BF),
            vmem((D, D), BF),
            vmem((NZ, NY, KB, 1), jnp.int32),
            vmem((NZ, NY, KB, 1), jnp.int32),
            vmem((NZ, NY, KB, D), BF),
            vmem((NZ, KB, D), BF),
            vmem((NZ, KB, D), BF),
            vmem((NZ, KB, D), BF),
            vmem((NZ, KB, D), BF),
            vmem((NZ, KB, D), BF),
            vmem((NZ, KB, D), BF),
            vmem((16, KB, D), BF),
            vmem((NY, KB, D), BF),
            vmem((NY, KB, D), BF),
            vmem((NY, 2, KB, HS), F32),
            vmem((3, KB, D), BF),
            vmem((3, 2, KB, HS), F32),
            vmem((24, NY, KB, D), BF),
            vmem((ROWS, 3 * D), BF),
            vmem((ROWS, D), F32),
            vmem((16, QB, HS), F32),
            vmem((16, QB, HS), F32),
            vmem((HEADS * 64, D), BF),
            vmem((256, D), BF),
            vmem((256, 2 * D), BF),
            vmem((ROWS, D), BF),
            pltpu.SemaphoreType.DMA((5,)),
            pltpu.SemaphoreType.DMA((COPIES,)),
            pltpu.SemaphoreType.DMA((COPIES,)),
        ],
        compiler_params=pltpu.CompilerParams(
            collective_id=0, has_side_effects=True, vmem_limit_bytes=54 * 1024 * 1024
        ),
    )(
        seg_start.reshape(4, 128), seg_end.reshape(4, 128), block_lists,
        tokens, w_qkv, w_coarse_out, w_kv2, w_out,
    )


def solution(mesh):
    placed = (
        P(("coarse", "fine"), None),
        P(),
        P(),
        P(),
        P(),
        P("coarse"),
        P("coarse"),
        P(("coarse", "fine"), None),
    )
    return jax.shard_map(
        body, mesh=mesh, in_specs=placed, out_specs=P(("coarse", "fine"), None), check_vma=False
    )
```

```python
import math

import jax
import jax.numpy as jnp
from jax import lax
from jax.experimental import pallas as pl
from jax.experimental.pallas import tpu as pltpu
from jax.sharding import PartitionSpec as P

HEADS = 8
KB = 16
QB = 256
NY = 4
NZ = 8
NC = 8
D = 1024
HS = 128
ROWS = 512
SEGS = 512
REACH = 256
SCALE = 1.0 / math.sqrt(HS)
SCALE2 = SCALE * math.log2(math.e)
BF = jnp.bfloat16
F32 = jnp.float32
NT = (((1,), (1,)), ((), ()))
MESH = pl.DeviceIdType.MESH


def dot(a, b):
    return jnp.dot(a, b, preferred_element_type=F32)


def dot_nt(a, b):
    return lax.dot_general(a, b, NT, preferred_element_type=F32)


def normalize(x):
    return x * lax.rsqrt(jnp.mean(x * x, axis=-1, keepdims=True) + 1e-06)


OFFS = (0, -1, 1, -2, 2, -3, 3, 4)
FAR = (-3, 3, 4)
COPIES = 31 + 24 + 95


def kernel(
    start_ref, end_ref, list_ref, tok_hbm, wqkv_hbm, wco_hbm, wkv2_hbm, wout_hbm,
    out_ref, tok, wqkv, wco, wkv2, wout, scol, ecol, part, rc, rd, re, relay, red, rz, t1, tq, po, pm, go, gm, t2, qkv, acc,
    mloc, lloc, qk, gath, kv2, att, load_sem, send_sem, recv_sem,
):
    c = lax.axis_index("coarse")
    f = lax.axis_index("fine")
    z = f // NY
    y = f % NY
    ya = y + 1 - 2 * (y % 2)
    yb = 3 - y
    yc = (y + 2) % 4
    up = (c + 1) % NC
    down = (c + NC - 1) % NC

    loads = [
        pltpu.make_async_copy(src, dst, load_sem.at[i])
        for i, (src, dst) in enumerate(
            ((tok_hbm, tok), (wqkv_hbm, wqkv), (wco_hbm, wco), (wkv2_hbm, wkv2), (wout_hbm, wout))
        )
    ]
    loads[0].start()

    at_y = lambda yy: {"fine": z * NY + yy}
    at_z = lambda zz: {"fine": zz * NY + y}
    at_c = lambda cc: {"coarse": cc}
    zat = lambda s: (z + s + NZ) % NZ

    barrier = pltpu.get_barrier_semaphore()
    peers = [at_z(zat(s)) for s in OFFS[1:]]
    peers += [at_y(ya), at_y(yb), at_y(yc), at_c(up), at_c(down)]
    for peer in peers:
        pl.semaphore_signal(barrier, inc=1, device_id=peer, device_id_type=MESH)

    copies = []

    def send(src, dst, where):
        k = len(copies)
        copy = pltpu.make_async_remote_copy(
            src_ref=src, dst_ref=dst, send_sem=send_sem.at[k], recv_sem=recv_sem.at[k],
            device_id=where, device_id_type=MESH,
        )
        copy.start()
        copies.append(copy)
        return copy

    first_row = (c * (NY * NZ) + f) * ROWS
    ends = jnp.concatenate([start_ref[...] - first_row, end_ref[...] - first_row], axis=0).T
    for k in range(4):
        scol[2 * k:2 * k + 2] = ends[:, k:k + 1].reshape(2, NY, KB, 1)
        ecol[2 * k:2 * k + 2] = ends[:, k + 4:k + 5].reshape(2, NY, KB, 1)

    forward = lambda s: s in (0, -1, -2, -3)
    via = lambda s: yb if forward(s) else ya
    other = lambda s: ya if forward(s) else yb
    slot = {s: i for i, s in enumerate(OFFS)}
    waits = {}

    def member_sums(pair):
        low, high = [], []
        for s in pair:
            for yy in (y, other(s), via(s), yc):
                low.append(scol[zat(s), yy])
                high.append(ecol[zat(s), yy])
        low = jnp.concatenate(low, axis=0)
        high = jnp.concatenate(high, axis=0)
        place = lax.broadcasted_iota(jnp.int32, (128, ROWS), 1)
        member = jnp.where((place >= low) & (place < high), 1.0, 0.0).astype(BF)
        sums = dot(member, tok[...]).astype(BF)
        for i, s in enumerate(pair):
            part[slot[s]] = sums[i * 64:(i + 1) * 64].reshape(NY, KB, D)

    def spread(pair):
        for s in pair:
            k = slot[s]
            waits["c", s] = send(part.at[k, 3], rc.at[k], at_y(via(s)))

    def pass_on(pair):
        for s in pair:
            k = slot[s]
            waits["c", s].wait_recv()
            relay[k] = (part[k, 1].astype(F32) + rc[k].astype(F32)).astype(BF)
            waits["e", s] = send(relay.at[k], re.at[k], at_y(other(s)))
        for s in pair:
            k = slot[s]
            waits["d", s] = send(part.at[k, 2], rd.at[k], at_y(via(s)))

    def settle(pair):
        for s in pair:
            k = slot[s]
            waits["d", s].wait_recv()
            waits["e", s].wait_recv()
            done = part[k, 0].astype(F32) + rd[k].astype(F32) + re[k].astype(F32)
            if s == 0:
                return done
            red[k] = done.astype(BF)
            waits["z", s] = send(red.at[k], rz.at[k], at_z(zat(s)))

    def project(j, carry):
        cols = pl.ds(pl.multiple_of(j * 256, 256), 256)
        qkv[:, cols] = dot(tok[...], wqkv[:, cols]).astype(BF)
        return carry

    def local(it, carry):
        rows = pl.ds(pl.multiple_of((it // HEADS) * QB, QB), QB)
        col = (it % HEADS) * HS
        cols = pl.ds(pl.multiple_of(col, HS), HS)
        keys = qkv[:, pl.ds(pl.multiple_of(col + D, HS), HS)]
        vals = qkv[:, pl.ds(pl.multiple_of(col + 2 * D, HS), HS)]
        s = dot_nt(qkv[rows, cols], keys)
        m = jnp.max(s, axis=1, keepdims=True)
        p = jnp.exp2((s - m) * SCALE2)
        lloc[it] = jnp.broadcast_to(jnp.sum(p, axis=1, keepdims=True), (QB, HS))
        mloc[it] = jnp.broadcast_to(m, (QB, HS))
        acc[rows, cols] = dot(p.astype(BF), vals)
        return carry

    projects = lambda a, b: lax.fori_loop(a, b, project, 0)
    locals_ = lambda a, b: lax.fori_loop(a, b, local, 0)

    pairs = (4, 3), (-3, 2), (-2, 1), (-1, 0)
    loads[0].wait()
    for load in loads[1:]:
        load.start()
    for pair in pairs:
        member_sums(pair)
    pl.semaphore_wait(barrier, len(peers))
    for pair in pairs:
        spread(pair)
    loads[1].wait()
    projects(0, 3)
    pass_on(pairs[0])
    pass_on(pairs[1])
    projects(3, 4)
    settle(pairs[0])
    pass_on(pairs[2])
    projects(4, 5)
    settle(pairs[1])
    pass_on(pairs[3])
    projects(5, 7)
    settle(pairs[2])
    projects(7, 9)
    total = settle(pairs[3])
    projects(9, 12)
    for s in OFFS[1:]:
        waits["z", s].wait_recv()
        total = total + rz[slot[s]].astype(F32)
    span = (ecol[z, y] - scol[z, y]).astype(F32)
    pooled = (total / jnp.sqrt(span)).astype(BF)
    t1[4 + z] = pooled
    tq[y] = pooled

    def across(zb):
        half = zb // 4
        spot = half * (zb - 4) + (1 - half) * (zb + 12)
        return send(t1.at[4 + zb], t1.at[spot], at_c((c + 2 * half + NC - 1) % NC))

    hops = {}
    rows_in = []
    for s in (1, -1, 4, 3, -3, 2, -2):
        hops[-s if s != 4 else 4] = send(t1.at[4 + z], t1.at[4 + z], at_z(zat(s)))
    for yy in (yc, ya, yb):
        rows_in.append(send(tq.at[y], tq.at[y], at_y(yy)))
    halo = [across(z)]
    for copy in rows_in:
        copy.wait_recv()

    query = dot(tq[...].reshape(64, D), wqkv[:, 0:D]).astype(BF)

    def absorb(h):
        qk[h * 64:(h + 1) * 64] = dot_nt(
            query[:, h * HS:(h + 1) * HS], wqkv[:, D + h * HS:D + (h + 1) * HS]
        ).astype(BF)

    absorb(0)
    absorb(1)
    for i, s in enumerate((-1, 1, -2, 2, -3, 3, 4)):
        hops[s].wait_recv()
        halo.append(across(zat(s)))
        if i < 6:
            absorb(2 + i)
    locals_(0, 5)
    for copy in halo:
        copy.wait_recv()

    table = t1[...].reshape(256, D)
    s = dot_nt(qk[...], table)
    row = z * 64 + lax.broadcasted_iota(jnp.int32, s.shape, 0) % 64
    place = lax.broadcasted_iota(jnp.int32, s.shape, 1)
    key = place // KB * 64 + place % KB + y * KB - REACH
    s = jnp.where(jnp.abs(row - key) <= REACH, s, -1e30)
    m = jnp.max(s, axis=1, keepdims=True)
    p = jnp.exp2((s - m) * SCALE2)
    l = jnp.sum(p, axis=1, keepdims=True)
    mixed = dot(p.astype(BF), table).astype(BF)
    lane = lax.broadcasted_iota(jnp.int32, (64, HS), 1)
    tops = jnp.zeros((64, HS), F32)
    sums = jnp.ones((64, HS), F32)
    for h in range(HEADS):
        rows = slice(h * 64, (h + 1) * 64)
        tops = jnp.where(lane == h, m[rows], tops)
        sums = jnp.where(lane == h, l[rows], sums)
        cols = slice(2 * D + h * HS, 2 * D + (h + 1) * HS)
        po[:, :, h * HS:(h + 1) * HS] = dot(mixed[rows], wqkv[:, cols]).astype(BF).reshape(
            NY, KB, HS
        )
    pm[:, 0] = tops.reshape(NY, KB, HS)
    pm[:, 1] = sums.reshape(NY, KB, HS)
    parts = []
    for j, yy in enumerate((yc, ya, yb)):
        parts.append(send(pm.at[yy], gm.at[j], at_y(yy)))
        parts.append(send(po.at[yy], go.at[j], at_y(yy)))
    locals_(5, 7)
    for copy in parts:
        copy.wait_recv()
    tops = [pm[y, 0]] + [gm[j, 0] for j in range(3)]
    sums = [pm[y, 1]] + [gm[j, 1] for j in range(3)]
    outs = [po[y].astype(F32)] + [go[j].astype(F32) for j in range(3)]
    peak = jnp.maximum(jnp.maximum(tops[0], tops[1]), jnp.maximum(tops[2], tops[3]))
    shares = [jnp.exp2((t - peak) * SCALE2) for t in tops]
    whole = sum(a * b for a, b in zip(shares, sums))
    shares = [a / whole for a in shares]
    mix = jnp.concatenate(
        [
            sum(a[:, h:h + 1] * o[:, h * HS:(h + 1) * HS] for a, o in zip(shares, outs))
            for h in range(HEADS)
        ],
        axis=1,
    ).astype(BF)
    loads[2].wait()
    state = normalize(dot(mix, wco[...])).astype(BF)
    t2[8 + z, y] = state
    near, turn, hops, halo = {}, {}, {}, []

    def over(zb, yy):
        src = t2.at[8 + zb, yy]
        halo.append(send(src, t2.at[zb, yy], at_c(up)))
        halo.append(send(src, t2.at[zb + 16, yy], at_c(down)))

    def alike(zb, yy, where):
        return send(t2.at[8 + zb, yy], t2.at[8 + zb, yy], where)

    def event(kind, s):
        zb = zat(s)
        if kind == "z":
            if s != 0:
                hops[s].wait_recv()
            near[s] = (alike(zb, y, at_y(ya)), alike(zb, y, at_y(yb)))
            if s in FAR:
                turn[s] = alike(zb, y, at_y(yc))
            over(zb, y)
        elif kind == "y":
            first, second = near[s]
            first.wait_recv()
            if forward(s) and s not in FAR:
                turn[s] = alike(zb, ya, at_y(yb))
            second.wait_recv()
            if not forward(s) and s not in FAR:
                turn[s] = alike(zb, yb, at_y(ya))
            over(zb, ya)
            over(zb, yb)
        elif kind == "c":
            turn[s].wait_recv()
            over(zb, yc)
        else:
            locals_(s, s + 1)

    for s in (1, -1, 4, 3, -3, 2, -2):
        hops[-s if s != 4 else 4] = alike(z, y, at_z(zat(s)))
    for kind, s in (
        ("z", 0), ("w", 7), ("w", 8), ("w", 9), ("w", 10), ("y", 0), ("z", -1), ("z", 1),
        ("w", 11), ("z", -2), ("z", 2), ("w", 12), ("c", 0), ("z", -3), ("z", 3), ("z", 4),
        ("y", -1), ("y", 1), ("w", 13), ("y", -2), ("y", 2), ("c", -1), ("c", 1), ("y", -3),
        ("y", 3), ("w", 14), ("c", -2), ("c", 2), ("y", 4), ("c", -3), ("c", 3), ("w", 15),
        ("c", 4),
    ):
        event(kind, s)
    for copy in halo:
        copy.wait_recv()

    for n in range(2):
        for j in range(8):
            rel = jnp.minimum((list_ref[n, j] - (c - 1) * 32 + 512) % 256, 95)
            k = n * 8 + j
            gath[k * KB:(k + 1) * KB] = t2[rel // NY, rel % NY]
    loads[3].wait()

    def second(j, carry):
        cols = pl.ds(pl.multiple_of(j * 256, 256), 256)
        kv2[:, cols] = dot(gath[...], wkv2[:, cols]).astype(BF)
        return carry

    lax.fori_loop(0, 8, second, 0)

    def remote(it, carry):
        n = it // HEADS
        rows = pl.ds(pl.multiple_of(n * QB, QB), QB)
        col = (it % HEADS) * HS
        cols = pl.ds(pl.multiple_of(col, HS), HS)
        listed = pl.ds(pl.multiple_of(n * 128, 128), 128)
        s = dot_nt(qkv[rows, cols], kv2[listed, cols])
        m0 = mloc[it]
        m = jnp.maximum(m0, jnp.max(s, axis=1, keepdims=True))
        a = jnp.exp2((m0 - m) * SCALE2)
        p = jnp.exp2((s - m) * SCALE2)
        total = a * lloc[it] + jnp.sum(p, axis=1, keepdims=True)
        vals = kv2[listed, pl.ds(pl.multiple_of(col + D, HS), HS)]
        o = acc[rows, cols] * a + dot(p.astype(BF), vals)
        att[rows, cols] = (o * (1.0 / total)).astype(BF)
        return carry

    lax.fori_loop(0, 16, remote, 0, unroll=8)
    loads[4].wait()

    def finish(i, carry):
        rows = pl.ds(pl.multiple_of(i * 256, 256), 256)
        out_ref[rows, :] = normalize(dot(att[rows, :], wout[...])).astype(BF)
        return carry

    lax.fori_loop(0, 2, finish, 0)
    for copy in copies:
        copy.wait_send()


def body(tokens, w_qkv, w_coarse_out, w_kv2, w_out, seg_start, seg_end, block_lists):
    vmem = lambda shape, kind: pltpu.VMEM(shape, kind)
    return pl.pallas_call(
        kernel,
        out_shape=jax.ShapeDtypeStruct((ROWS, D), BF),
        in_specs=[
            pl.BlockSpec(memory_space=pltpu.VMEM),
            pl.BlockSpec(memory_space=pltpu.VMEM),
            pl.BlockSpec(memory_space=pltpu.SMEM),
        ] + [pl.BlockSpec(memory_space=pltpu.HBM)] * 5,
        out_specs=pl.BlockSpec(memory_space=pltpu.VMEM),
        scratch_shapes=[
            vmem((ROWS, D), BF),
            vmem((D, 3 * D), BF),
            vmem((D, D), BF),
            vmem((D, 2 * D), BF),
            vmem((D, D), BF),
            vmem((NZ, NY, KB, 1), jnp.int32),
            vmem((NZ, NY, KB, 1), jnp.int32),
            vmem((NZ, NY, KB, D), BF),
            vmem((NZ, KB, D), BF),
            vmem((NZ, KB, D), BF),
            vmem((NZ, KB, D), BF),
            vmem((NZ, KB, D), BF),
            vmem((NZ, KB, D), BF),
            vmem((NZ, KB, D), BF),
            vmem((16, KB, D), BF),
            vmem((NY, KB, D), BF),
            vmem((NY, KB, D), BF),
            vmem((NY, 2, KB, HS), F32),
            vmem((3, KB, D), BF),
            vmem((3, 2, KB, HS), F32),
            vmem((24, NY, KB, D), BF),
            vmem((ROWS, 3 * D), BF),
            vmem((ROWS, D), F32),
            vmem((16, QB, HS), F32),
            vmem((16, QB, HS), F32),
            vmem((HEADS * 64, D), BF),
            vmem((256, D), BF),
            vmem((256, 2 * D), BF),
            vmem((ROWS, D), BF),
            pltpu.SemaphoreType.DMA((5,)),
            pltpu.SemaphoreType.DMA((COPIES,)),
            pltpu.SemaphoreType.DMA((COPIES,)),
        ],
        compiler_params=pltpu.CompilerParams(
            collective_id=0, has_side_effects=True, vmem_limit_bytes=52 * 1024 * 1024
        ),
    )(
        seg_start.reshape(4, 128), seg_end.reshape(4, 128), block_lists,
        tokens, w_qkv, w_coarse_out, w_kv2, w_out,
    )


def solution(mesh):
    placed = (
        P(("coarse", "fine"), None),
        P(),
        P(),
        P(),
        P(),
        P("coarse"),
        P("coarse"),
        P(("coarse", "fine"), None),
    )
    return jax.shard_map(
        body, mesh=mesh, in_specs=placed, out_specs=P(("coarse", "fine"), None), check_vma=False
    )
```

```python
import math

import jax
import jax.numpy as jnp
from jax import lax
from jax.experimental import pallas as pl
from jax.experimental.pallas import tpu as pltpu
from jax.sharding import PartitionSpec as P

HEADS = 8
KB = 16
QB = 256
NY = 4
NZ = 8
NC = 8
D = 1024
HS = 128
ROWS = 512
SEGS = 512
REACH = 256
SCALE = 1.0 / math.sqrt(HS)
SCALE2 = SCALE * math.log2(math.e)
BF = jnp.bfloat16
F32 = jnp.float32
NT = (((1,), (1,)), ((), ()))
MESH = pl.DeviceIdType.MESH


def dot(a, b):
    return jnp.dot(a, b, preferred_element_type=F32)


def dot_nt(a, b):
    return lax.dot_general(a, b, NT, preferred_element_type=F32)


def normalize(x):
    return x * lax.rsqrt(jnp.mean(x * x, axis=-1, keepdims=True) + 1e-06)


OFFS = (0, -1, 1, -2, 2, -3, 3, 4)
COPIES = 31 + 24 + 95


def kernel(
    start_ref, end_ref, list_ref, tok_hbm, wqkv_hbm, wco_hbm, wkv2_hbm, wout_hbm,
    out_ref, tok, wqkv, wco, wkv2, wout, scol, ecol, part, rc, rd, re, relay, red, rz, t1, vcol, tq, po, pm, go, gm, t2, qkv, acc,
    mloc, lloc, qk, gath, kv2, att, load_sem, send_sem, recv_sem,
):
    c = lax.axis_index("coarse")
    f = lax.axis_index("fine")
    z = f // NY
    y = f % NY
    ya = y + 1 - 2 * (y % 2)
    yb = 3 - y
    yc = (y + 2) % 4
    up = (c + 1) % NC
    down = (c + NC - 1) % NC

    loads = [
        pltpu.make_async_copy(src, dst, load_sem.at[i])
        for i, (src, dst) in enumerate(
            ((tok_hbm, tok), (wqkv_hbm, wqkv), (wco_hbm, wco), (wkv2_hbm, wkv2), (wout_hbm, wout))
        )
    ]
    loads[0].start()

    at_y = lambda yy: {"fine": z * NY + yy}
    at_z = lambda zz: {"fine": zz * NY + y}
    at_c = lambda cc: {"coarse": cc}
    zat = lambda s: (z + s + NZ) % NZ

    barrier = pltpu.get_barrier_semaphore()
    peers = [at_z(zat(s)) for s in OFFS[1:]]
    peers += [at_y(ya), at_y(yb), at_y(yc), at_c(up), at_c(down)]
    for peer in peers:
        pl.semaphore_signal(barrier, inc=1, device_id=peer, device_id_type=MESH)

    copies = []

    def send(src, dst, where):
        k = len(copies)
        copy = pltpu.make_async_remote_copy(
            src_ref=src, dst_ref=dst, send_sem=send_sem.at[k], recv_sem=recv_sem.at[k],
            device_id=where, device_id_type=MESH,
        )
        copy.start()
        copies.append(copy)
        return copy

    first_row = (c * (NY * NZ) + f) * ROWS
    ends = jnp.concatenate([start_ref[...] - first_row, end_ref[...] - first_row], axis=0).T
    for k in range(4):
        scol[2 * k:2 * k + 2] = ends[:, k:k + 1].reshape(2, NY, KB, 1)
        ecol[2 * k:2 * k + 2] = ends[:, k + 4:k + 5].reshape(2, NY, KB, 1)

    forward = lambda s: s in (0, -1, -2, -3)
    via = lambda s: yb if forward(s) else ya
    other = lambda s: ya if forward(s) else yb
    slot = {s: i for i, s in enumerate(OFFS)}
    waits = {}

    def member_sums(pair):
        low, high = [], []
        for s in pair:
            for yy in (y, other(s), via(s), yc):
                low.append(scol[zat(s), yy])
                high.append(ecol[zat(s), yy])
        low = jnp.concatenate(low, axis=0)
        high = jnp.concatenate(high, axis=0)
        place = lax.broadcasted_iota(jnp.int32, (128, ROWS), 1)
        member = jnp.where((place >= low) & (place < high), 1.0, 0.0).astype(BF)
        sums = dot(member, tok[...]).astype(BF)
        for i, s in enumerate(pair):
            part[slot[s]] = sums[i * 64:(i + 1) * 64].reshape(NY, KB, D)

    def spread(pair):
        for s in pair:
            k = slot[s]
            waits["c", s] = send(part.at[k, 3], rc.at[k], at_y(via(s)))

    def pass_on(pair):
        for s in pair:
            k = slot[s]
            waits["c", s].wait_recv()
            relay[k] = (part[k, 1].astype(F32) + rc[k].astype(F32)).astype(BF)
            waits["e", s] = send(relay.at[k], re.at[k], at_y(other(s)))
        for s in pair:
            k = slot[s]
            waits["d", s] = send(part.at[k, 2], rd.at[k], at_y(via(s)))

    def settle(pair):
        for s in pair:
            k = slot[s]
            waits["d", s].wait_recv()
            waits["e", s].wait_recv()
            done = part[k, 0].astype(F32) + rd[k].astype(F32) + re[k].astype(F32)
            if s == 0:
                return done
            red[k] = done.astype(BF)
            waits["z", s] = send(red.at[k], rz.at[k], at_z(zat(s)))

    def project(j, carry):
        cols = pl.ds(pl.multiple_of(j * 256, 256), 256)
        qkv[:, cols] = dot(tok[...], wqkv[:, cols]).astype(BF)
        return carry

    def local(it, carry):
        rows = pl.ds(pl.multiple_of((it // HEADS) * QB, QB), QB)
        col = (it % HEADS) * HS
        cols = pl.ds(pl.multiple_of(col, HS), HS)
        keys = qkv[:, pl.ds(pl.multiple_of(col + D, HS), HS)]
        vals = qkv[:, pl.ds(pl.multiple_of(col + 2 * D, HS), HS)]
        s = dot_nt(qkv[rows, cols], keys)
        m = jnp.max(s, axis=1, keepdims=True)
        p = jnp.exp2((s - m) * SCALE2)
        lloc[it] = jnp.broadcast_to(jnp.sum(p, axis=1, keepdims=True), (QB, HS))
        mloc[it] = jnp.broadcast_to(m, (QB, HS))
        acc[rows, cols] = dot(p.astype(BF), vals)
        return carry

    projects = lambda a, b: lax.fori_loop(a, b, project, 0)
    locals_ = lambda a, b: lax.fori_loop(a, b, local, 0)

    pairs = (4, 3), (-3, 2), (-2, 1), (-1, 0)
    loads[0].wait()
    for load in loads[1:]:
        load.start()
    for pair in pairs:
        member_sums(pair)
    pl.semaphore_wait(barrier, len(peers))
    for pair in pairs:
        spread(pair)
    loads[1].wait()
    projects(0, 3)
    pass_on(pairs[0])
    pass_on(pairs[1])
    projects(3, 4)
    settle(pairs[0])
    pass_on(pairs[2])
    projects(4, 5)
    settle(pairs[1])
    pass_on(pairs[3])
    projects(5, 7)
    settle(pairs[2])
    projects(7, 9)
    total = settle(pairs[3])
    projects(9, 12)
    for s in OFFS[1:]:
        waits["z", s].wait_recv()
        total = total + rz[slot[s]].astype(F32)
    span = (ecol[z, y] - scol[z, y]).astype(F32)
    pooled = (total / jnp.sqrt(span)).astype(BF)
    t1[4 + z] = pooled
    tq[y] = pooled

    def across(zb):
        half = zb // 4
        spot = half * (zb - 4) + (1 - half) * (zb + 12)
        return send(t1.at[4 + zb], t1.at[spot], at_c((c + 2 * half + NC - 1) % NC))

    hops = {}
    rows_in = []
    for s in (1, -1, 4, 3, -3, 2, -2):
        hops[-s if s != 4 else 4] = send(t1.at[4 + z], t1.at[4 + z], at_z(zat(s)))
    for yy in (yc, ya, yb):
        rows_in.append(send(tq.at[y], tq.at[y], at_y(yy)))
    halo = [across(z)]
    for copy in rows_in:
        copy.wait_recv()

    query = dot(tq[...].reshape(64, D), wqkv[:, 0:D]).astype(BF)

    def absorb(h):
        qk[h * 64:(h + 1) * 64] = dot_nt(
            query[:, h * HS:(h + 1) * HS], wqkv[:, D + h * HS:D + (h + 1) * HS]
        ).astype(BF)

    absorb(0)
    absorb(1)
    for i, s in enumerate((-1, 1, -2, 2, -3, 3, 4)):
        hops[s].wait_recv()
        halo.append(across(zat(s)))
        if i < 6:
            absorb(2 + i)
    half = (8, KB, D)
    vcol[4:12] = dot(t1[4:12].reshape(128, D), wqkv[:, 2 * D:3 * D]).astype(BF).reshape(half)
    locals_(0, 3)
    for copy in halo:
        copy.wait_recv()

    table = t1[...].reshape(256, D)
    s = dot_nt(qk[...], table)
    edges = jnp.concatenate([table[0:64], table[192:256]], axis=0)
    edges = dot(edges, wqkv[:, 2 * D:3 * D]).astype(BF)
    vcol[0:4] = edges[0:64].reshape(4, KB, D)
    vcol[12:16] = edges[64:128].reshape(4, KB, D)
    row = z * 64 + lax.broadcasted_iota(jnp.int32, s.shape, 0) % 64
    place = lax.broadcasted_iota(jnp.int32, s.shape, 1)
    key = place // KB * 64 + place % KB + y * KB - REACH
    s = jnp.where(jnp.abs(row - key) <= REACH, s, -1e30)
    m = jnp.max(s, axis=1, keepdims=True)
    p = jnp.exp2((s - m) * SCALE2)
    l = jnp.sum(p, axis=1, keepdims=True)
    values = vcol[...].reshape(256, D)
    p = p.astype(BF)
    lane = lax.broadcasted_iota(jnp.int32, (64, HS), 1)
    tops = jnp.zeros((64, HS), F32)
    sums = jnp.ones((64, HS), F32)
    for h in range(HEADS):
        rows = slice(h * 64, (h + 1) * 64)
        tops = jnp.where(lane == h, m[rows], tops)
        sums = jnp.where(lane == h, l[rows], sums)
        cols = slice(h * HS, (h + 1) * HS)
        po[:, :, cols] = dot(p[rows], values[:, cols]).astype(BF).reshape(
            NY, KB, HS
        )
    pm[:, 0] = tops.reshape(NY, KB, HS)
    pm[:, 1] = sums.reshape(NY, KB, HS)
    parts = []
    for j, yy in enumerate((yc, ya, yb)):
        parts.append(send(pm.at[yy], gm.at[j], at_y(yy)))
        parts.append(send(po.at[yy], go.at[j], at_y(yy)))
    locals_(3, 7)
    for copy in parts:
        copy.wait_recv()
    tops = [pm[y, 0]] + [gm[j, 0] for j in range(3)]
    sums = [pm[y, 1]] + [gm[j, 1] for j in range(3)]
    outs = [po[y].astype(F32)] + [go[j].astype(F32) for j in range(3)]
    peak = jnp.maximum(jnp.maximum(tops[0], tops[1]), jnp.maximum(tops[2], tops[3]))
    shares = [jnp.exp2((t - peak) * SCALE2) for t in tops]
    whole = sum(a * b for a, b in zip(shares, sums))
    shares = [a / whole for a in shares]
    mix = jnp.concatenate(
        [
            sum(a[:, h:h + 1] * o[:, h * HS:(h + 1) * HS] for a, o in zip(shares, outs))
            for h in range(HEADS)
        ],
        axis=1,
    ).astype(BF)
    loads[2].wait()
    state = normalize(dot(mix, wco[...])).astype(BF)
    t2[8 + z, y] = state
    near, turn, hops, halo = {}, {}, {}, []

    def over(zb, yy):
        src = t2.at[8 + zb, yy]
        halo.append(send(src, t2.at[zb, yy], at_c(up)))
        halo.append(send(src, t2.at[zb + 16, yy], at_c(down)))

    def alike(zb, yy, where):
        return send(t2.at[8 + zb, yy], t2.at[8 + zb, yy], where)

    def event(kind, s):
        zb = zat(s)
        if kind == "z":
            if s != 0:
                hops[s].wait_recv()
            near[s] = (alike(zb, y, at_y(ya)), alike(zb, y, at_y(yb)))
            over(zb, y)
        elif kind == "y":
            first, second = near[s]
            first.wait_recv()
            if forward(s):
                turn[s] = alike(zb, ya, at_y(yb))
            second.wait_recv()
            if not forward(s):
                turn[s] = alike(zb, yb, at_y(ya))
            over(zb, ya)
            over(zb, yb)
        elif kind == "c":
            turn[s].wait_recv()
            over(zb, yc)
        else:
            locals_(s, s + 1)

    for s in (1, -1, 4, 3, -3, 2, -2):
        hops[-s if s != 4 else 4] = alike(z, y, at_z(zat(s)))
    for kind, s in (
        ("z", 0), ("w", 7), ("w", 8), ("w", 9), ("w", 10), ("y", 0), ("z", -1), ("z", 1),
        ("w", 11), ("z", -2), ("z", 2), ("w", 12), ("c", 0), ("z", -3), ("z", 3), ("z", 4),
        ("y", -1), ("y", 1), ("w", 13), ("y", -2), ("y", 2), ("c", -1), ("c", 1), ("y", -3),
        ("y", 3), ("w", 14), ("c", -2), ("c", 2), ("y", 4), ("c", -3), ("c", 3), ("w", 15),
        ("c", 4),
    ):
        event(kind, s)
    for copy in halo:
        copy.wait_recv()

    for n in range(2):
        for j in range(8):
            rel = jnp.minimum((list_ref[n, j] - (c - 1) * 32 + 512) % 256, 95)
            k = n * 8 + j
            gath[k * KB:(k + 1) * KB] = t2[rel // NY, rel % NY]
    loads[3].wait()

    def second(j, carry):
        cols = pl.ds(pl.multiple_of(j * 512, 512), 512)
        kv2[:, cols] = dot(gath[...], wkv2[:, cols]).astype(BF)
        return carry

    lax.fori_loop(0, 4, second, 0)

    def remote(it, carry):
        n = it // HEADS
        rows = pl.ds(pl.multiple_of(n * QB, QB), QB)
        col = (it % HEADS) * HS
        cols = pl.ds(pl.multiple_of(col, HS), HS)
        listed = pl.ds(pl.multiple_of(n * 128, 128), 128)
        s = dot_nt(qkv[rows, cols], kv2[listed, cols])
        m0 = mloc[it]
        m = jnp.maximum(m0, jnp.max(s, axis=1, keepdims=True))
        a = jnp.exp2((m0 - m) * SCALE2)
        p = jnp.exp2((s - m) * SCALE2)
        total = a * lloc[it] + jnp.sum(p, axis=1, keepdims=True)
        vals = kv2[listed, pl.ds(pl.multiple_of(col + D, HS), HS)]
        o = acc[rows, cols] * a + dot(p.astype(BF), vals)
        att[rows, cols] = (o * (1.0 / total)).astype(BF)
        return carry

    lax.fori_loop(0, 16, remote, 0, unroll=8)
    loads[4].wait()

    def finish(i, carry):
        rows = pl.ds(pl.multiple_of(i * 256, 256), 256)
        out_ref[rows, :] = normalize(dot(att[rows, :], wout[...])).astype(BF)
        return carry

    lax.fori_loop(0, 2, finish, 0)
    for copy in copies:
        copy.wait_send()


def body(tokens, w_qkv, w_coarse_out, w_kv2, w_out, seg_start, seg_end, block_lists):
    vmem = lambda shape, kind: pltpu.VMEM(shape, kind)
    return pl.pallas_call(
        kernel,
        out_shape=jax.ShapeDtypeStruct((ROWS, D), BF),
        in_specs=[
            pl.BlockSpec(memory_space=pltpu.VMEM),
            pl.BlockSpec(memory_space=pltpu.VMEM),
            pl.BlockSpec(memory_space=pltpu.SMEM),
        ] + [pl.BlockSpec(memory_space=pltpu.HBM)] * 5,
        out_specs=pl.BlockSpec(memory_space=pltpu.VMEM),
        scratch_shapes=[
            vmem((ROWS, D), BF),
            vmem((D, 3 * D), BF),
            vmem((D, D), BF),
            vmem((D, 2 * D), BF),
            vmem((D, D), BF),
            vmem((NZ, NY, KB, 1), jnp.int32),
            vmem((NZ, NY, KB, 1), jnp.int32),
            vmem((NZ, NY, KB, D), BF),
            vmem((NZ, KB, D), BF),
            vmem((NZ, KB, D), BF),
            vmem((NZ, KB, D), BF),
            vmem((NZ, KB, D), BF),
            vmem((NZ, KB, D), BF),
            vmem((NZ, KB, D), BF),
            vmem((16, KB, D), BF),
            vmem((16, KB, D), BF),
            vmem((NY, KB, D), BF),
            vmem((NY, KB, D), BF),
            vmem((NY, 2, KB, HS), F32),
            vmem((3, KB, D), BF),
            vmem((3, 2, KB, HS), F32),
            vmem((24, NY, KB, D), BF),
            vmem((ROWS, 3 * D), BF),
            vmem((ROWS, D), F32),
            vmem((16, QB, HS), F32),
            vmem((16, QB, HS), F32),
            vmem((HEADS * 64, D), BF),
            vmem((256, D), BF),
            vmem((256, 2 * D), BF),
            vmem((ROWS, D), BF),
            pltpu.SemaphoreType.DMA((5,)),
            pltpu.SemaphoreType.DMA((COPIES,)),
            pltpu.SemaphoreType.DMA((COPIES,)),
        ],
        compiler_params=pltpu.CompilerParams(
            collective_id=0, has_side_effects=True, vmem_limit_bytes=54 * 1024 * 1024
        ),
    )(
        seg_start.reshape(4, 128), seg_end.reshape(4, 128), block_lists,
        tokens, w_qkv, w_coarse_out, w_kv2, w_out,
    )


def solution(mesh):
    placed = (
        P(("coarse", "fine"), None),
        P(),
        P(),
        P(),
        P(),
        P("coarse"),
        P("coarse"),
        P(("coarse", "fine"), None),
    )
    return jax.shard_map(
        body, mesh=mesh, in_specs=placed, out_specs=P(("coarse", "fine"), None), check_vma=False
    )
```
